32 devices in a mesh: dp: 8 (over z, x), tensor: 4 (over y, core).
Axes of the slice: x: 2, y: 2, z: 4, core: 2. Of those that a mesh axis runs over, the one named last changes fastest.
Arguments:
- tokens_in: bfloat16 [16384, 1152], P(('dp', 'tensor')), may hold values from -6 to 6
- condition: bfloat16 [16, 1152], P('dp'), may hold values from -6 to 6
- w_ada: bfloat16 [1152, 6912], P('dp', 'tensor'), may hold values from -0.1875 to 0.1875
- b_ada: bfloat16 [6912], P('tensor'), may hold values from -3 to 3
- w_qkv: bfloat16 [1152, 3456], P('dp', 'tensor'), may hold values from -0.1875 to 0.1875
- b_qv: bfloat16 [2304], P('tensor'), may hold values from -3 to 3
- w_proj: bfloat16 [1152, 1152], P('tensor', 'dp'), may hold values from -2 to 2
- b_proj: bfloat16 [1152], replicated, may hold values from -3 to 3
- w_fc1: bfloat16 [1152, 4608], P('dp', 'tensor'), may hold values from -0.1875 to 0.1875
- b_fc1: bfloat16 [4608], P('tensor'), may hold values from -3 to 3
- w_fc2: bfloat16 [4608, 1152], P('tensor', 'dp'), may hold values from -0.09375 to 0.09375
- b_fc2: bfloat16 [1152], replicated, may hold values from -3 to 3
- cotangent: bfloat16 [16384, 1152], P(('dp', 'tensor')), may hold values from -6 to 6
Outputs:
- block_out: bfloat16 [16384, 1152], P(('dp', 'tensor'))
- grad_tokens: float32 [16384, 1152], P(('dp', 'tensor'))
- grad_condition: float32 [16, 1152], P('dp')
- grad_w_ada: float32 [1152, 6912], P('dp', 'tensor')
- grad_b_ada: float32 [6912], P('tensor')
- grad_w_qkv: float32 [1152, 3456], P('dp', 'tensor')
- grad_b_qv: float32 [2304], P('tensor')
- grad_w_proj: float32 [1152, 1152], P('tensor', 'dp')
- grad_b_proj: float32 [1152], replicated
- grad_w_fc1: float32 [1152, 4608], P('dp', 'tensor')
- grad_b_fc1: float32 [4608], P('tensor')
- grad_w_fc2: float32 [4608, 1152], P('tensor', 'dp')
- grad_b_fc2: float32 [1152], replicated
The draws below stay inside these ranges and needn't reach their ends.
All inputs are finite; a program needn't handle non-finite values.
Results may differ from the reference program's by a relative error of at most 0.015.
The reference program's roundings to bfloat16 on the way count: a program that leaves them out, or rounds other values in their place, can miss the bound.
Values may be sent and summed in bfloat16 or wider, within the bound.
No kernel may reach another device: no remote copies, remote signals or barrier semaphores. Data moves between devices by JAX's collectives and lax.ppermute only.
A program may use at most 192 MiB of HBM per device.

```python
import math
import jax
import jax.numpy as jnp
from jax import lax

D = 1152
HEADS = 16
HEAD_DIM = 72
FF = 4608
SEQ = 1024
LATENTS = 16
TOKENS = 16384


def level_of(own_key, extent, shards, low, largest):
    loudness = 1.0
    for axis_at, blocks in shards:
        steps = jax.random.uniform(jax.random.fold_in(jax.random.fold_in(own_key, 6), axis_at), (blocks,), jnp.float32, low / len(shards), largest / len(shards))
        loudness = loudness * jnp.repeat(jnp.exp(steps), extent[axis_at] // blocks).reshape((-1,) + (1,) * (len(extent) - 1 - axis_at))
    return loudness


def scatter_about(key, dims, deviation, limit, cuts=(), kind=jnp.bfloat16):
    level = level_of(key, dims, cuts, -0.22, 0.18) if cuts else 1.0
    values = jax.random.normal(key, dims, jnp.float32) * deviation * level
    return jnp.minimum(jnp.maximum(values, -limit), limit).astype(kind)


def setup_inputs(seed: int = 0) -> dict:
    streams_of = jax.random.split(jax.random.key(seed), 14)
    tokens_in = scatter_about(streams_of[0], (TOKENS, D), 1.0, 6.0, ((0, 32),))
    condition = scatter_about(streams_of[1], (LATENTS, D), 1.0, 6.0, ((0, 8),))
    w_ada = scatter_about(streams_of[2], (D, 6 * D), D ** -0.5, 0.1875, ((0, 8), (1, 4)))
    b_ada = scatter_about(streams_of[3], (6 * D,), 0.5, 3.0, ((0, 4),))
    w_qkv = scatter_about(streams_of[4], (D, 3 * D), D ** -0.5, 0.1875, ((0, 8), (1, 4)))
    b_qv = scatter_about(streams_of[5], (2 * D,), 0.5, 3.0, ((0, 4),))
    w_proj = scatter_about(streams_of[6], (D, D), (max(D // 128, 1)) ** -0.5, 2.0, ((0, 4), (1, 8)))
    b_proj = scatter_about(streams_of[7], (D,), 0.5, 3.0)
    w_fc1 = scatter_about(streams_of[8], (D, FF), D ** -0.5, 0.1875, ((0, 8), (1, 4)))
    b_fc1 = scatter_about(streams_of[9], (FF,), 0.5, 3.0, ((0, 4),))
    w_fc2 = scatter_about(streams_of[10], (FF, D), FF ** -0.5, 0.09375, ((0, 4), (1, 8)))
    b_fc2 = scatter_about(streams_of[11], (D,), 0.5, 3.0)
    cotangent = scatter_about(streams_of[12], (TOKENS, D), 1.0, 6.0, ((0, 32),))
    return dict(tokens_in=tokens_in, condition=condition, w_ada=w_ada, b_ada=b_ada, w_qkv=w_qkv, b_qv=b_qv, w_proj=w_proj, b_proj=b_proj, w_fc1=w_fc1, b_fc1=b_fc1, w_fc2=w_fc2, b_fc2=b_fc2, cotangent=cotangent)


@jax.custom_vjp
def low(v):
    return lax.optimization_barrier(v.astype(jnp.bfloat16)).astype(jnp.float32)

@jax.custom_vjp
def low_back(v):
    return v

def low_keep(v):
    return (low(v), None)

def low_pass(kept, grad):
    return (grad,)

def back_keep(v):
    return (v, None)

def back_low(kept, grad):
    return (low(grad),)
low.defvjp(low_keep, low_pass)
low_back.defvjp(back_keep, back_low)
highest = lax.Precision.HIGHEST

def layer_norm(values):
    row_mean = lax.optimization_barrier(jnp.mean(values, axis=-1, keepdims=True))
    centre = values - row_mean
    row_var = lax.optimization_barrier(jnp.mean(centre * centre, axis=-1, keepdims=True))
    return centre * lax.rsqrt(row_var + 1e-06)

def gelu_tanh(values):
    return 0.5 * values * (1.0 + jnp.tanh(0.7978845608028654 * (values + 0.044715 * values * values * values)))

def attend(operands):
    queries, keys_r, values_r = operands
    scores = low_back(jnp.einsum('qhd,khd->hqk', queries, keys_r, precision=highest) * HEAD_DIM ** (-0.5))
    attn_probs = low(jax.nn.softmax(scores, axis=-1))
    return jnp.einsum('hqk,khd->qhd', attn_probs, values_r, precision=highest)

def block(tokens_val, cond_val, w_ada, b_ada, w_qkv, b_qv, w_proj, b_proj, w_fc1, b_fc1, w_fc2, b_fc2):
    group_size = cond_val.shape[0]
    row_total = tokens_val.shape[0]
    modulation = jnp.dot(low(jax.nn.silu(cond_val)), w_ada, precision=highest) + b_ada
    mod_rows = jnp.repeat(modulation, SEQ, axis=0)
    shift_attn, scale_attn, gate_attn, shift_mlp, scale_mlp, gate_mlp = jnp.split(mod_rows, 6, axis=1)
    attn_in = low(layer_norm(tokens_val) * (1.0 + scale_attn) + shift_attn)
    projected = jnp.dot(attn_in, w_qkv, precision=highest).reshape(row_total, HEADS, 3, HEAD_DIM)
    bias_qv = b_qv.reshape(HEADS, 2, HEAD_DIM)
    queries = low_back(low(projected[:, :, 0] + bias_qv[:, 0]))
    keys_r = low_back(low(projected[:, :, 1]))
    values_r = low_back(low(projected[:, :, 2] + bias_qv[:, 1]))
    block_shape = (group_size, SEQ, HEADS, HEAD_DIM)
    mixture = lax.map(jax.checkpoint(attend), (queries.reshape(block_shape), keys_r.reshape(block_shape), values_r.reshape(block_shape)))
    mixture = low_back(low(mixture.reshape(row_total, D)))
    attn_out = low_back(jnp.dot(mixture, w_proj, precision=highest) + b_proj)
    middle = tokens_val + gate_attn * attn_out
    mlp_in = low(layer_norm(middle) * (1.0 + scale_mlp) + shift_mlp)
    pre_act = low_back(jnp.dot(mlp_in, w_fc1, precision=highest) + b_fc1)
    activated = low(gelu_tanh(pre_act))
    mlp_out = low_back(jnp.dot(activated, w_fc2, precision=highest) + b_fc2)
    return middle + gate_mlp * mlp_out

def reference(tokens_in, condition, w_ada, b_ada, w_qkv, b_qv, w_proj, b_proj, w_fc1, b_fc1, w_fc2, b_fc2, cotangent):
    weights = tuple((weight_arg.astype(jnp.float32) for weight_arg in (w_ada, b_ada, w_qkv, b_qv, w_proj, b_proj, w_fc1, b_fc1, w_fc2, b_fc2)))
    group_size = math.gcd(LATENTS, 4)
    scan_steps = LATENTS // group_size
    token_groups = tokens_in.astype(jnp.float32).reshape(scan_steps, group_size * SEQ, D)
    cond_groups = condition.astype(jnp.float32).reshape(scan_steps, group_size, D)
    grad_groups = cotangent.astype(jnp.float32).reshape(scan_steps, group_size * SEQ, D)

    def one_group(running, group_item):
        tokens_val, cond_val, grad_val = group_item
        result, pull_back = jax.vjp(block, tokens_val, cond_val, *weights)
        gradients = pull_back(grad_val)
        running = tuple((total_sum + group_sum for total_sum, group_sum in zip(running, gradients[2:])))
        return (running, (result.astype(jnp.bfloat16), gradients[0], gradients[1]))
    zero_sums = tuple((jnp.zeros(weight_arg.shape, jnp.float32) for weight_arg in weights))
    totals, (outputs, grad_tok, grad_cond) = lax.scan(one_group, zero_sums, (token_groups, cond_groups, grad_groups))
    return (outputs.reshape(TOKENS, D), grad_tok.reshape(TOKENS, D), grad_cond.reshape(LATENTS, D), totals[0], totals[1], totals[2], totals[3], totals[4], totals[5], totals[6], totals[7], totals[8], totals[9])
```

```python
import jax
import jax.numpy as jnp
from jax import lax
from jax.experimental import pallas as pl
from jax.experimental.pallas import tpu as pltpu
from jax.sharding import PartitionSpec as P

HEAD_DIM = 72
SEQ = 1024

highest = lax.Precision.HIGHEST
root_two_pi = 0.7978845608028654
cubic_term = 0.044715
epsilon = 1e-06
bf16 = jnp.bfloat16
f32 = jnp.float32


def normalize(values):
    centre = values - jnp.mean(values, axis=-1, keepdims=True)
    inverse = lax.rsqrt(jnp.mean(centre * centre, axis=-1, keepdims=True) + epsilon)
    return (centre * inverse, inverse)


def norm_back(normed, inverse, grad_in):
    mean_grad = jnp.mean(grad_in, axis=-1, keepdims=True)
    mean_cross = jnp.mean(grad_in * normed, axis=-1, keepdims=True)
    return inverse * (grad_in - mean_grad - normed * mean_cross)


def gelu_parts(pre_act):
    tangent = jnp.tanh(root_two_pi * (pre_act + cubic_term * pre_act * pre_act * pre_act))
    activated = 0.5 * pre_act * (1.0 + tangent)
    gelu_slope = 0.5 * (1.0 + tangent) + 0.5 * pre_act * (1.0 - tangent * tangent) * root_two_pi * (
        1.0 + 3.0 * cubic_term * pre_act * pre_act
    )
    return (activated, gelu_slope)


def swap_cores(values):
    return lax.ppermute(values, "tensor", [(i, i ^ 1) for i in range(4)])


def swap_y(values):
    return lax.ppermute(values, "tensor", [(i, i ^ 2) for i in range(4)])


def swap_dp(values, bit):
    size = lax.axis_size("dp")
    return lax.ppermute(values, "dp", [(i, i ^ (1 << bit)) for i in range(size)])


def place_blocks(pieces, order_bits):
    half, rows, _ = pieces[0][0].shape
    widths = [first.shape[2] for first, _ in pieces]
    total = sum(widths)
    dp = 2 * half

    def rel_of(j, me):
        apart = j ^ me
        rel = 0
        for place, bit in enumerate(order_bits):
            rel = rel | (((apart >> bit) & 1) << place)
        return rel

    def kernel(me_ref, *refs):
        out_ref = refs[-1]
        rel = rel_of(pl.program_id(0), me_ref[0])

        @pl.when(rel < half)
        def _():
            at = 0
            for i, n in enumerate(widths):
                out_ref[0, :, at : at + n] = refs[2 * i][0]
                at += n

        @pl.when(rel >= half)
        def _():
            at = 0
            for i, n in enumerate(widths):
                out_ref[0, :, at : at + n] = refs[2 * i + 1][0]
                at += n

    def first_map(j, me_ref):
        rel = rel_of(j, me_ref[0])
        return (jnp.where(rel < half, rel, 0), 0, 0)

    def second_map(j, me_ref):
        rel = rel_of(j, me_ref[0])
        return (jnp.where(rel >= half, rel - half, 0), 0, 0)

    in_specs = []
    operands = []
    for (first, second), n in zip(pieces, widths):
        in_specs += [pl.BlockSpec((1, rows, n), first_map), pl.BlockSpec((1, rows, n), second_map)]
        operands += [first, second]
    me = lax.axis_index("dp").astype(jnp.int32).reshape(1)
    placed = pl.pallas_call(
        kernel,
        out_shape=jax.ShapeDtypeStruct((dp, rows, total), bf16),
        grid_spec=pltpu.PrefetchScalarGridSpec(
            num_scalar_prefetch=1,
            grid=(dp,),
            in_specs=in_specs,
            out_specs=pl.BlockSpec((1, rows, total), lambda j, me_ref: (j, 0, 0)),
        ),
        cost_estimate=pl.CostEstimate(flops=0, transcendentals=0, bytes_accessed=5 * dp * rows * total),
        name="place_blocks",
    )(me, *operands)
    return placed.reshape(dp * rows, total)


def gather_group(shard, cut):
    dp = lax.axis_size("dp")
    bits = dp.bit_length() - 1
    order_bits = list(range(bits - 1, -1, -1))
    got = shard[None]
    for bit in order_bits[:-1]:
        got = jnp.concatenate([got, swap_dp(got, bit)], axis=0)
    last = order_bits[-1]
    part_a, part_b = got[:, :, :cut], got[:, :, cut:]
    a_x = swap_dp(part_a, last)
    b_y = swap_y(part_b)
    a_both = swap_y(jnp.concatenate([part_a, a_x], axis=0))
    b_both = swap_dp(jnp.concatenate([part_b, b_y], axis=0), last)
    half = dp // 2
    pieces = [
        (part_a, a_x),
        (part_b, b_both[:half]),
        (a_both[:half], a_both[half:]),
        (b_y, b_both[half:]),
    ]
    return place_blocks(pieces, order_bits)


def scatter_half(own, other, y_first):
    dp = lax.axis_size("dp")
    me = lax.axis_index("dp")
    bits = dp.bit_length() - 1
    rows = own.shape[0] // dp
    n = own.shape[1]

    own = own.astype(f32)
    if y_first:
        total = own + swap_y(other.astype(bf16)).astype(f32)
        blocks = total.reshape(dp // 2, 2, rows, n)
        keep = lax.dynamic_index_in_dim(blocks, me & 1, 1, False)
        send = lax.dynamic_index_in_dim(blocks, 1 - (me & 1), 1, False)
        total = keep + swap_dp(send.astype(bf16), 0).astype(f32)
    else:
        both = jnp.stack([own, other.astype(f32)]).reshape(2, dp // 2, 2, rows, n)
        keep = lax.dynamic_index_in_dim(both, me & 1, 2, False)
        send = lax.dynamic_index_in_dim(both, 1 - (me & 1), 2, False)
        both = keep + swap_dp(send.astype(bf16), 0).astype(f32)
        total = both[0] + swap_y(both[1].astype(bf16)).astype(f32)
    for bit in range(1, bits):
        count = total.shape[0]
        blocks = total.reshape(count // 2, 2, rows, n)
        mine = (me >> bit) & 1
        keep = lax.dynamic_index_in_dim(blocks, mine, 1, False)
        send = lax.dynamic_index_in_dim(blocks, 1 - mine, 1, False)
        total = keep + swap_dp(send.astype(bf16), bit).astype(f32)
    return total[0]


def scatter_group(left, right, cut):
    n = right.shape[1] // 2

    def term(lo, hi, kind):
        out = lax.dot_general(
            left, right[:, lo:hi], (((0,), (0,)), ((), ())), preferred_element_type=f32
        )
        return out.astype(kind)

    part_a = scatter_half(term(0, cut, f32), term(n, n + cut, bf16), True)
    part_b = scatter_half(term(cut, n, f32), term(n + cut, 2 * n, f32), False)
    return jnp.concatenate([part_a, part_b], axis=1)


def dot_nt(left_rows, right_mat):
    return lax.dot_general(
        left_rows, right_mat, (((1,), (1,)), ((), ())), preferred_element_type=f32
    )


def dot_nn(left_rows, right_mat):
    return jnp.dot(left_rows, right_mat, preferred_element_type=f32)


def flip_halves(values):
    half = values.shape[0] // 2
    return jnp.concatenate([values[half:], values[:half]], axis=0)


def sum_cores_all(partial):
    mine = partial.astype(bf16)
    theirs = flip_halves(swap_cores(mine))
    return mine.astype(f32) + theirs.astype(f32)


def sum_cores_own(partial):
    mine = partial.astype(bf16)
    half = mine.shape[0] // 2
    theirs = swap_cores(mine[half:])
    return mine[:half].astype(f32) + theirs.astype(f32)


def attend(queries, keys_b, values_b):
    score_scale = queries.shape[-1] ** (-0.5)
    scores = (
        jnp.einsum("qhd,khd->hqk", queries, keys_b, preferred_element_type=f32) * score_scale
    )
    row_max = jnp.max(scores, axis=-1, keepdims=True)
    exponent = jnp.exp(scores - row_max)
    row_total = jnp.sum(exponent, axis=-1, keepdims=True)
    attn_probs = (exponent / row_total).astype(bf16)
    mixture = jnp.einsum("hqk,khd->qhd", attn_probs, values_b, preferred_element_type=f32)
    return (mixture.astype(bf16), (row_max + jnp.log(row_total))[..., 0])


def attend_back(queries, keys_b, values_b, grad_mix, logsum):
    score_scale = queries.shape[-1] ** (-0.5)
    scores = (
        jnp.einsum("qhd,khd->hqk", queries, keys_b, preferred_element_type=f32) * score_scale
    )
    attn_probs = jnp.exp(scores - logsum[..., None])
    grad_probs = jnp.einsum("qhd,khd->hqk", grad_mix, values_b, preferred_element_type=f32)
    row_inner = jnp.sum(grad_probs * attn_probs, axis=-1, keepdims=True)
    grad_scores = (attn_probs * (grad_probs - row_inner)).astype(bf16)
    grad_queries = (
        jnp.einsum("hqk,khd->qhd", grad_scores, keys_b, preferred_element_type=f32) * score_scale
    )
    grad_keys = (
        jnp.einsum("hqk,qhd->khd", grad_scores, queries, preferred_element_type=f32) * score_scale
    )
    grad_values = jnp.einsum(
        "hqk,qhd->khd", attn_probs.astype(bf16), grad_mix, preferred_element_type=f32
    )
    return jnp.stack([grad_queries, grad_keys, grad_values], axis=2).astype(bf16)


def shards(
    tokens_in,
    condition,
    w_ada,
    b_ada,
    w_qkv,
    b_qv,
    w_proj,
    b_proj,
    w_fc1,
    b_fc1,
    w_fc2,
    b_fc2,
    cotangent,
):
    tok_rows, width = tokens_in.shape
    head_size = HEAD_DIM
    dp_at = lax.axis_index("dp")
    y_at = lax.axis_index("tensor") // 2
    t_at = lax.axis_index("tensor")
    dp_size = lax.axis_size("dp")
    ada_rows, ada_cols = w_ada.shape
    n_qkv, n_proj, n_fc1, n_fc2 = w_qkv.shape[1], w_proj.shape[0], w_fc1.shape[1], w_fc2.shape[0]

    tokens_all = jnp.concatenate([tokens_in, swap_cores(tokens_in)], axis=0)
    cot_all = jnp.concatenate([cotangent, swap_cores(cotangent)], axis=0)
    bias_mine = jnp.concatenate([b_qv, b_fc1])
    bias_theirs = swap_y(bias_mine)
    n_bqv = b_qv.shape[0]

    wqkv = gather_group(w_qkv, 384)
    group_two = gather_group(jnp.concatenate([w_proj.T, w_fc1], axis=1), 672)
    n_two = n_proj + n_fc1
    wproj_t = jnp.concatenate([group_two[:, :n_proj], group_two[:, n_two : n_two + n_proj]], axis=1)
    wfc1 = jnp.concatenate([group_two[:, n_proj:n_two], group_two[:, n_two + n_proj :]], axis=1)
    wfc2_t = gather_group(w_fc2.T, 512)

    cond_all = lax.all_gather(condition, "dp", axis=0, tiled=True).astype(f32)
    silu_all = (cond_all * jax.nn.sigmoid(cond_all)).astype(bf16)
    silu_mine = lax.dynamic_slice_in_dim(silu_all, dp_at * ada_rows, ada_rows, 1)
    mod_part = jnp.dot(silu_mine, w_ada, preferred_element_type=f32)
    mod_cols = lax.psum_scatter(mod_part, "dp", scatter_dimension=0, tiled=True) + b_ada.astype(f32)
    modulation = lax.all_gather(mod_cols, "tensor", axis=1, tiled=True)
    mod_row = lax.dynamic_slice_in_dim(modulation, y_at, 1, 0)
    shift_attn, scale_attn, gate_attn, shift_mlp, scale_mlp, gate_mlp = jnp.split(mod_row, 6, axis=1)

    input_vals = tokens_all.astype(f32)
    normed_one, inverse_one = normalize(input_vals)
    attn_in = (normed_one * (1.0 + scale_attn) + shift_attn).astype(bf16)
    heads = 2 * n_qkv // (3 * head_size)
    rows = 2 * tok_rows
    bias_qv = jnp.concatenate([bias_mine[:n_bqv], bias_theirs[:n_bqv]]).astype(f32).reshape(heads, 2, head_size)
    projected = dot_nn(attn_in, wqkv).reshape(rows, heads, 3, head_size)
    queries = (projected[:, :, 0] + bias_qv[:, 0]).astype(bf16)
    keys_b = projected[:, :, 1].astype(bf16)
    values_b = (projected[:, :, 2] + bias_qv[:, 1]).astype(bf16)
    mixture, logsum = attend(queries, keys_b, values_b)
    mix_rows = mixture.reshape(rows, heads * head_size)
    attn_out = sum_cores_all(dot_nt(mix_rows, wproj_t)) + b_proj.astype(f32)
    middle = input_vals + gate_attn * attn_out

    normed_two, inverse_two = normalize(middle)
    mlp_in = (normed_two * (1.0 + scale_mlp) + shift_mlp).astype(bf16)
    bias_one = jnp.concatenate([bias_mine[n_bqv:], bias_theirs[n_bqv:]]).astype(f32)
    pre_act = dot_nn(mlp_in, wfc1) + bias_one
    activated, gelu_slope = gelu_parts(pre_act)
    act_rows = activated.astype(bf16)
    mlp_out = sum_cores_own(dot_nt(act_rows, wfc2_t)) + b_fc2.astype(f32)
    result = middle[:tok_rows] + gate_mlp * mlp_out

    grad_out = cot_all.astype(f32)
    grad_mlp = (gate_mlp * grad_out).astype(bf16)
    d_gate_mlp = grad_out[:tok_rows] * mlp_out
    grad_act = dot_nn(grad_mlp, wfc2_t)
    grad_pre = (grad_act * gelu_slope).astype(bf16)
    owned_fc2 = scatter_group(grad_mlp, act_rows, 512).T
    owned_fc1 = scatter_group(mlp_in, grad_pre, 512)
    grad_mlp_in = sum_cores_all(dot_nt(grad_pre, wfc1))
    d_scale_mlp = grad_mlp_in * normed_two
    grad_middle = grad_out + norm_back(normed_two, inverse_two, grad_mlp_in * (1.0 + scale_mlp))

    grad_attn = (gate_attn * grad_middle).astype(bf16)
    d_gate_attn = grad_middle * attn_out
    grad_mix = dot_nn(grad_attn, wproj_t).astype(bf16).reshape(rows, heads, head_size)
    owned_proj = scatter_group(grad_attn, mix_rows, 128).T
    grad_qkv = attend_back(queries, keys_b, values_b, grad_mix, logsum).reshape(rows, 2 * n_qkv)
    owned_qkv = scatter_group(attn_in, grad_qkv, 384)
    grad_attn_in = sum_cores_own(dot_nt(grad_qkv, wqkv))
    d_scale_attn = grad_attn_in * normed_one[:tok_rows]
    grad_tokens = grad_middle[:tok_rows] + norm_back(
        normed_one[:tok_rows], inverse_one[:tok_rows], grad_attn_in * (1.0 + scale_attn)
    )

    own = [
        jnp.sum(term[:tok_rows], axis=0)
        for term in (grad_attn_in, d_scale_attn, d_gate_attn, grad_mlp_in, d_scale_mlp, d_gate_mlp)
    ]
    mod_sums = jnp.concatenate(own)
    mod_sums = mod_sums + swap_cores(mod_sums)
    by_rank = mod_sums.reshape(4, ada_cols)
    mod_keep = lax.dynamic_index_in_dim(by_rank, t_at, 0, True)
    mod_got = swap_y(lax.dynamic_index_in_dim(by_rank, t_at ^ 2, 0, True))
    first = jnp.where(y_at == 0, mod_keep, mod_got)
    second = jnp.where(y_at == 0, mod_got, mod_keep)
    grad_mod = lax.all_gather(jnp.concatenate([first, second], axis=0), "dp", axis=0, tiled=True)
    owned_ada = lax.dot_general(
        silu_mine.astype(f32), grad_mod, (((0,), (0,)), ((), ())), precision=highest
    )
    grad_ba = jnp.sum(grad_mod, axis=0)
    silu_part = lax.dot_general(
        grad_mod, w_ada.astype(f32), (((1,), (1,)), ((), ())), precision=highest
    )
    silu_place = lax.dynamic_update_slice(
        jnp.zeros((silu_part.shape[0], width), f32), silu_part, (0, dp_at * ada_rows)
    )

    qkv_sums = jnp.sum(grad_qkv.astype(f32), axis=0).reshape(2, heads // 2, 3, head_size)
    bqv_two = jnp.stack([qkv_sums[:, :, 0], qkv_sums[:, :, 2]], axis=2).reshape(2, n_bqv)
    b1_two = jnp.sum(grad_pre.astype(f32), axis=0).reshape(2, n_fc1)
    two = jnp.concatenate([bqv_two, b1_two], axis=1)
    bias_place = lax.dynamic_update_slice(jnp.zeros((4, two.shape[1]), f32), two[:1], (t_at, 0))
    bias_place = lax.dynamic_update_slice(bias_place, two[1:], (t_at ^ 2, 0))
    grad_bo = jnp.sum(grad_attn[:tok_rows].astype(f32), axis=0)
    grad_b2 = jnp.sum(grad_mlp[:tok_rows].astype(f32), axis=0)
    silu_total, bias_total, grad_bo, grad_b2 = lax.psum(
        (silu_place, bias_place, grad_bo, grad_b2), ("dp", "tensor")
    )
    bias_own = lax.dynamic_index_in_dim(bias_total, t_at, 0, False)
    cond_vals = condition.astype(f32)
    cond_sigmoid = jax.nn.sigmoid(cond_vals)
    latents = condition.shape[0]
    grad_silu = lax.dynamic_slice_in_dim(silu_total, dp_at * latents, latents, 0)
    grad_condition = grad_silu * cond_sigmoid * (1.0 + cond_vals * (1.0 - cond_sigmoid))
    return (
        result.astype(bf16),
        grad_tokens,
        grad_condition,
        owned_ada,
        grad_ba,
        owned_qkv,
        bias_own[:n_bqv],
        owned_proj,
        grad_bo,
        owned_fc1,
        bias_own[n_bqv:],
        owned_fc2,
        grad_b2,
    )


def solution(mesh):
    placed = (
        P(("dp", "tensor"), None),
        P("dp", None),
        P("dp", "tensor"),
        P("tensor"),
        P("dp", "tensor"),
        P("tensor"),
        P("tensor", "dp"),
        P(),
        P("dp", "tensor"),
        P("tensor"),
        P("tensor", "dp"),
        P(),
        P(("dp", "tensor"), None),
    )
    return jax.shard_map(
        shards,
        mesh=mesh,
        in_specs=placed,
        out_specs=(
            P(("dp", "tensor"), None),
            P(("dp", "tensor"), None),
            P("dp", None),
            P("dp", "tensor"),
            P("tensor"),
            P("dp", "tensor"),
            P("tensor"),
            P("tensor", "dp"),
            P(),
            P("dp", "tensor"),
            P("tensor"),
            P("tensor", "dp"),
            P(),
        ),
        check_vma=False,
    )
```

```python
import jax
import jax.numpy as jnp
from jax import lax
from jax.experimental import pallas as pl
from jax.experimental.pallas import tpu as pltpu
from jax.sharding import PartitionSpec as P

HEAD_DIM = 72
SEQ = 1024

highest = lax.Precision.HIGHEST
root_two_pi = 0.7978845608028654
cubic_term = 0.044715
epsilon = 1e-06
log2_e = 1.4426950408889634
bf16 = jnp.bfloat16
f32 = jnp.float32


def normalize(values):
    centre = values - jnp.mean(values, axis=-1, keepdims=True)
    inverse = lax.rsqrt(jnp.mean(centre * centre, axis=-1, keepdims=True) + epsilon)
    return (centre * inverse, inverse)


def norm_back(normed, inverse, grad_in):
    mean_grad = jnp.mean(grad_in, axis=-1, keepdims=True)
    mean_cross = jnp.mean(grad_in * normed, axis=-1, keepdims=True)
    return inverse * (grad_in - mean_grad - normed * mean_cross)


def gelu_parts(pre_act):
    tangent = jnp.tanh(root_two_pi * (pre_act + cubic_term * pre_act * pre_act * pre_act))
    activated = 0.5 * pre_act * (1.0 + tangent)
    gelu_slope = 0.5 * (1.0 + tangent) + 0.5 * pre_act * (1.0 - tangent * tangent) * root_two_pi * (
        1.0 + 3.0 * cubic_term * pre_act * pre_act
    )
    return (activated, gelu_slope)


def swap_cores(values):
    return lax.ppermute(values, "tensor", [(i, i ^ 1) for i in range(4)])


def swap_y(values):
    return lax.ppermute(values, "tensor", [(i, i ^ 2) for i in range(4)])


def swap_dp(values, bit):
    size = lax.axis_size("dp")
    return lax.ppermute(values, "dp", [(i, i ^ (1 << bit)) for i in range(size)])


def after(values, *deps):
    return lax.optimization_barrier((values, deps))[0]


def dp_bits():
    return lax.axis_size("dp").bit_length() - 1


def own_bit(bit):
    return (lax.axis_index("dp") >> bit) & 1


def ordered(flag, mine, theirs, axis):
    first = jnp.where(flag == 0, mine, theirs)
    second = jnp.where(flag == 0, theirs, mine)
    return jnp.concatenate([first, second], axis=axis)


def gather_small(values):
    for bit in range(dp_bits()):
        values = ordered(own_bit(bit), values, swap_dp(values, bit), 0)
    return values


def scatter_small(values):
    for bit in reversed(range(dp_bits())):
        halves = values.reshape((2, values.shape[0] // 2) + values.shape[1:])
        mine = own_bit(bit)
        keep = lax.dynamic_index_in_dim(halves, mine, 0, False)
        send = lax.dynamic_index_in_dim(halves, 1 - mine, 0, False)
        values = keep + swap_dp(send, bit)
    return values


def exchange_small(values):
    dp, k, n = values.shape
    values = values[:, :, None]
    for bit in range(dp_bits()):
        pairs = values.reshape((values.shape[0] // 2, 2) + values.shape[1:])
        mine = own_bit(bit)
        keep = lax.dynamic_index_in_dim(pairs, mine, 1, False)
        send = lax.dynamic_index_in_dim(pairs, 1 - mine, 1, False)
        values = ordered(mine, keep, swap_dp(send, bit), 2)
    return values.reshape(k, dp * n)


def place_blocks(pieces, outputs, order_bits):
    half, rows, _ = pieces[0][0].shape
    widths = [first.shape[2] for first, _ in pieces]
    totals = [sum(hi - lo for _, lo, hi in spec) for spec in outputs]
    dp = 2 * half

    def rel_of(j, me):
        apart = j ^ me
        rel = 0
        for place, bit in enumerate(order_bits):
            rel = rel | (((apart >> bit) & 1) << place)
        return rel

    def kernel(me_ref, *refs):
        rel = rel_of(pl.program_id(0), me_ref[0])
        out_refs = refs[2 * len(pieces) :]

        def write(which):
            for out_ref, spec in zip(out_refs, outputs):
                at = 0
                for i, lo, hi in spec:
                    out_ref[0, :, at : at + hi - lo] = refs[2 * i + which][0, :, lo:hi]
                    at += hi - lo

        @pl.when(rel < half)
        def _():
            write(0)

        @pl.when(rel >= half)
        def _():
            write(1)

    def first_map(j, me_ref):
        rel = rel_of(j, me_ref[0])
        return (jnp.where(rel < half, rel, 0), 0, 0)

    def second_map(j, me_ref):
        rel = rel_of(j, me_ref[0])
        return (jnp.where(rel >= half, rel - half, 0), 0, 0)

    in_specs = []
    operands = []
    for (first, second), n in zip(pieces, widths):
        in_specs += [pl.BlockSpec((1, rows, n), first_map), pl.BlockSpec((1, rows, n), second_map)]
        operands += [first, second]
    me = lax.axis_index("dp").astype(jnp.int32).reshape(1)
    placed = pl.pallas_call(
        kernel,
        out_shape=[jax.ShapeDtypeStruct((dp, rows, total), bf16) for total in totals],
        grid_spec=pltpu.PrefetchScalarGridSpec(
            num_scalar_prefetch=1,
            grid=(dp,),
            in_specs=in_specs,
            out_specs=[
                pl.BlockSpec((1, rows, total), lambda j, me_ref: (j, 0, 0)) for total in totals
            ],
        ),
        cost_estimate=pl.CostEstimate(
            flops=0, transcendentals=0, bytes_accessed=5 * dp * rows * sum(totals)
        ),
        name="place_blocks",
    )(me, *operands)
    return [array.reshape(dp * rows, total) for array, total in zip(placed, totals)]


def gather_start(shard):
    got = shard[None]
    for bit in range(dp_bits() - 1, 0, -1):
        got = jnp.concatenate([got, swap_dp(got, bit)], axis=0)
    return got


def gather_end(got, cut, outputs):
    half = got.shape[0]
    part_a, part_b = got[:, :, :cut], got[:, :, cut:]
    a_x = swap_dp(part_a, 0)
    b_y = swap_y(part_b)
    a_both = swap_y(jnp.concatenate([part_a, a_x], axis=0))
    b_both = swap_dp(jnp.concatenate([part_b, b_y], axis=0), 0)
    pieces = [
        (part_a, a_x),
        (part_b, b_both[:half]),
        (a_both[:half], a_both[half:]),
        (b_y, b_both[half:]),
    ]
    columns = []
    for spec in outputs:
        split = []
        for far, lo, hi in spec:
            if lo < cut:
                split.append((2 * far, lo, min(hi, cut)))
            if hi > cut:
                split.append((2 * far + 1, max(lo, cut) - cut, hi - cut))
        columns.append(split)
    return place_blocks(pieces, columns, list(range(dp_bits() - 1, -1, -1)))


def split_bit(blocks, axis, bit):
    mine = own_bit(bit)
    keep = lax.dynamic_index_in_dim(blocks, mine, axis, False)
    send = lax.dynamic_index_in_dim(blocks, 1 - mine, axis, False)
    return keep, send.astype(bf16)


def weight_term(left, right, kind):
    out = lax.dot_general(left, right, (((0,), (0,)), ((), ())), preferred_element_type=f32)
    dp = lax.axis_size("dp")
    return out.astype(kind).reshape(dp // 2, 2, out.shape[0] // dp, out.shape[1])


def low_stages(total, deps):
    for bit in range(1, dp_bits()):
        blocks = total.reshape((total.shape[0] // 2, 2) + total.shape[1:])
        keep, send = split_bit(blocks, 1, bit)
        got = swap_dp(send, bit)
        if deps:
            got = after(got, deps.pop(0))
        total = keep + got.astype(f32)
    return total[0]


def y_first_send(far):
    return swap_y(far)


def y_first_mid(near, got):
    keep, send = split_bit(near + got.astype(f32), 1, 0)
    return keep, swap_dp(send, 0)


def x_first_send(near, far):
    keep_near, send_near = split_bit(near, 1, 0)
    keep_far, send_far = split_bit(far, 1, 0)
    return keep_near, keep_far, swap_dp(jnp.stack([send_near, send_far]), 0)


def x_first_mid(keep_near, keep_far, got):
    far = (keep_far + got[1].astype(f32)).astype(bf16)
    return keep_near + got[0].astype(f32), swap_y(far)


def dot_nt(left_rows, right_mat):
    return lax.dot_general(
        left_rows, right_mat, (((1,), (1,)), ((), ())), preferred_element_type=f32
    )


def dot_nn(left_rows, right_mat):
    return jnp.dot(left_rows, right_mat, preferred_element_type=f32)


def flip_halves(values):
    half = values.shape[0] // 2
    return jnp.concatenate([values[half:], values[:half]], axis=0)


def sum_cores_all(partial):
    mine = partial.astype(bf16)
    theirs = flip_halves(swap_cores(mine))
    return mine.astype(f32) + theirs.astype(f32)


def sum_cores_own(partial):
    mine = partial.astype(bf16)
    half = mine.shape[0] // 2
    theirs = swap_cores(mine[half:])
    return mine[:half].astype(f32) + theirs.astype(f32)


def attend(qkv, block=512, unroll=2):
    rows, cols = qkv.shape
    size = HEAD_DIM
    heads = cols // (3 * size)
    factor = size ** (-0.5) * log2_e

    def kernel(x_ref, mix_ref, lse_ref, q_s, k_s, v_s, o_s, l_s):
        i = pl.program_id(0)

        @pl.when(i == 0)
        def _():
            for h in range(heads):
                b = h * 3 * size
                q_s[h] = x_ref[:, b : b + size]
                k_s[h] = x_ref[:, b + size : b + 2 * size]
                v_s[h] = x_ref[:, b + 2 * size : b + 3 * size]

        def one(h):
            q = q_s[h, pl.ds(pl.multiple_of(i * block, block), block), :]
            scores = lax.dot_general(
                q, k_s[h], (((1,), (1,)), ((), ())), preferred_element_type=f32
            )
            top = jnp.max(scores, axis=-1, keepdims=True)
            probs = jnp.exp2((scores - top) * factor)
            total = jnp.sum(probs, axis=-1, keepdims=True)
            out = jnp.dot(probs.astype(bf16), v_s[h], preferred_element_type=f32)
            o_s[h] = (out / total).astype(bf16)
            l_s[h] = top * factor + jnp.log2(total)

        def body(g, _):
            for u in range(unroll):
                one(g * unroll + u)
            return 0

        lax.fori_loop(0, heads // unroll, body, 0)
        for h in range(heads):
            mix_ref[:, h * size : (h + 1) * size] = o_s[h]
            lse_ref[:, h : h + 1] = l_s[h]

    return pl.pallas_call(
        kernel,
        out_shape=(
            jax.ShapeDtypeStruct((rows, heads * size), bf16),
            jax.ShapeDtypeStruct((rows, heads), f32),
        ),
        grid=(rows // block,),
        in_specs=[pl.BlockSpec((rows, cols), lambda i: (0, 0))],
        out_specs=(
            pl.BlockSpec((block, heads * size), lambda i: (i, 0)),
            pl.BlockSpec((block, heads), lambda i: (i, 0)),
        ),
        scratch_shapes=[pltpu.VMEM((heads, rows, size), bf16)] * 3
        + [pltpu.VMEM((heads, block, size), bf16), pltpu.VMEM((heads, block, 1), f32)],
        compiler_params=pltpu.CompilerParams(vmem_limit_bytes=48 << 20),
        cost_estimate=pl.CostEstimate(
            flops=16 * heads * rows * rows * size,
            transcendentals=heads * rows * rows,
            bytes_accessed=rows * cols * 2 + rows * heads * size * 2,
        ),
        name="attend",
    )(qkv)


def attend_back(qkv, grad_mix, lse, first, heads, block=512, unroll=2):
    rows, cols = qkv.shape
    size = HEAD_DIM
    all_heads = cols // (3 * size)
    factor = size ** (-0.5) * log2_e
    scale = size ** (-0.5)
    steps = rows // block

    def kernel(x_ref, g_ref, lse_ref, out_ref, q_s, k_s, v_s, g_s, dq_s, dk_s, dv_s):
        i = pl.program_id(0)

        @pl.when(i == 0)
        def _():
            for h in range(heads):
                b = (first + h) * 3 * size
                q_s[h] = x_ref[:, b : b + size]
                k_s[h] = x_ref[:, b + size : b + 2 * size]
                v_s[h] = x_ref[:, b + 2 * size : b + 3 * size]
                g_s[h] = g_ref[:, (first + h) * size : (first + h + 1) * size]
            dk_s[...] = jnp.zeros_like(dk_s)
            dv_s[...] = jnp.zeros_like(dv_s)

        at = pl.ds(pl.multiple_of(i * block, block), block)

        def one(h):
            q = q_s[h, at, :]
            g = g_s[h, at, :]
            k = k_s[h]
            scores = lax.dot_general(k, q, (((1,), (1,)), ((), ())), preferred_element_type=f32)
            probs = jnp.exp2(scores * factor - lse_ref[first + h, :, at])
            grad_probs = lax.dot_general(
                v_s[h], g, (((1,), (1,)), ((), ())), preferred_element_type=f32
            )
            inner = jnp.sum(probs * grad_probs, axis=0, keepdims=True)
            grad_scores = (probs * (grad_probs - inner)).astype(bf16)
            dv_s[h] += jnp.dot(probs.astype(bf16), g, preferred_element_type=f32)
            dk_s[h] += jnp.dot(grad_scores, q, preferred_element_type=f32)
            grad_q = lax.dot_general(
                grad_scores, k, (((0,), (0,)), ((), ())), preferred_element_type=f32
            )
            dq_s[h, at, :] = (grad_q * scale).astype(bf16)

        def body(g, _):
            for u in range(unroll):
                one(g * unroll + u)
            return 0

        lax.fori_loop(0, heads // unroll, body, 0)

        @pl.when(i == steps - 1)
        def _():
            for h in range(heads):
                b = h * 3 * size
                out_ref[:, b : b + size] = dq_s[h]
                out_ref[:, b + size : b + 2 * size] = (dk_s[h] * scale).astype(bf16)
                out_ref[:, b + 2 * size : b + 3 * size] = dv_s[h].astype(bf16)

    return pl.pallas_call(
        kernel,
        out_shape=jax.ShapeDtypeStruct((rows, heads * 3 * size), bf16),
        grid=(steps,),
        in_specs=[
            pl.BlockSpec((rows, cols), lambda i: (0, 0)),
            pl.BlockSpec((rows, all_heads * size), lambda i: (0, 0)),
            pl.BlockSpec((all_heads, 1, rows), lambda i: (0, 0, 0)),
        ],
        out_specs=pl.BlockSpec((rows, heads * 3 * size), lambda i: (0, 0)),
        scratch_shapes=[pltpu.VMEM((heads, rows, size), bf16)] * 5
        + [pltpu.VMEM((heads, rows, size), f32)] * 2,
        compiler_params=pltpu.CompilerParams(vmem_limit_bytes=56 << 20),
        cost_estimate=pl.CostEstimate(
            flops=40 * heads * rows * rows * size,
            transcendentals=heads * rows * rows,
            bytes_accessed=rows * cols * 4,
        ),
        name="attend_back",
    )(qkv, grad_mix, lse)


def shards(
    tokens_in,
    condition,
    w_ada,
    b_ada,
    w_qkv,
    b_qv,
    w_proj,
    b_proj,
    w_fc1,
    b_fc1,
    w_fc2,
    b_fc2,
    cotangent,
):
    tok_rows, width = tokens_in.shape
    head_size = HEAD_DIM
    dp_at = lax.axis_index("dp")
    y_at = lax.axis_index("tensor") // 2
    t_at = lax.axis_index("tensor")
    dp_size = lax.axis_size("dp")
    ada_rows, ada_cols = w_ada.shape
    n_qkv, n_proj, n_fc1, n_fc2 = w_qkv.shape[1], w_proj.shape[0], w_fc1.shape[1], w_fc2.shape[0]

    tokens_all = jnp.concatenate([tokens_in, swap_cores(tokens_in)], axis=0)
    cot_all = jnp.concatenate([cotangent, swap_cores(cotangent)], axis=0)
    bias_mine = jnp.concatenate([b_qv, b_fc1])
    bias_theirs = swap_y(bias_mine)
    n_bqv = b_qv.shape[0]

    got_qkv = gather_start(w_qkv)
    got_two = gather_start(after(jnp.concatenate([w_fc1[:, :384], w_proj.T, w_fc1[:, 384:]], axis=1), got_qkv))
    got_fc2 = gather_start(after(w_fc2.T, got_two))
    (wqkv,) = gather_end(got_qkv, 384, [[(0, 0, n_qkv), (1, 0, n_qkv)]])
    fc1_at = 384 + n_proj
    end_two = n_fc1 + n_proj
    wproj_t, wfc1 = gather_end(
        got_two,
        fc1_at,
        [
            [(0, 384, fc1_at), (1, 384, fc1_at)],
            [(0, 0, 384), (0, fc1_at, end_two), (1, 0, 384), (1, fc1_at, end_two)],
        ],
    )
    (wfc2_t,) = gather_end(got_fc2, 512, [[(0, 0, n_fc2), (1, 0, n_fc2)]])

    cond_all = gather_small(condition).astype(f32)
    silu_all = (cond_all * jax.nn.sigmoid(cond_all)).astype(bf16)
    silu_mine = lax.dynamic_slice_in_dim(silu_all, dp_at * ada_rows, ada_rows, 1)
    mod_part = jnp.dot(silu_mine, w_ada, preferred_element_type=f32)
    mod_cols = scatter_small(mod_part) + b_ada.astype(f32)
    mod_mine = lax.dynamic_slice_in_dim(mod_cols, y_at, 1, 0)
    mod_near = swap_y(lax.dynamic_slice_in_dim(mod_cols, 1 - y_at, 1, 0))
    core_at = t_at % 2
    mod_two = ordered(y_at, mod_mine, mod_near, 0)
    mod_row = ordered(core_at, mod_two[:, None], swap_cores(mod_two)[:, None], 1).reshape(1, 4 * ada_cols)
    shift_attn, scale_attn, gate_attn, shift_mlp, scale_mlp, gate_mlp = jnp.split(mod_row, 6, axis=1)

    input_vals = tokens_all.astype(f32)
    normed_one, inverse_one = normalize(input_vals)
    attn_in = (normed_one * (1.0 + scale_attn) + shift_attn).astype(bf16)
    heads = 2 * n_qkv // (3 * head_size)
    bias_qv = jnp.concatenate([bias_mine[:n_bqv], bias_theirs[:n_bqv]]).reshape(heads, 2, head_size)
    bias_qkv = jnp.stack([bias_qv[:, 0], jnp.zeros_like(bias_qv[:, 0]), bias_qv[:, 1]], axis=1)
    qkv = (dot_nn(attn_in, wqkv) + bias_qkv.astype(f32).reshape(1, 2 * n_qkv)).astype(bf16)
    mix_rows, lse = attend(qkv)
    attn_out = sum_cores_all(dot_nt(mix_rows, wproj_t)) + b_proj.astype(f32)
    middle = input_vals + gate_attn * attn_out

    normed_two, inverse_two = normalize(middle)
    mlp_in = (normed_two * (1.0 + scale_mlp) + shift_mlp).astype(bf16)
    bias_one = jnp.concatenate([bias_mine[n_bqv:], bias_theirs[n_bqv:]]).astype(f32)
    pre_act = dot_nn(mlp_in, wfc1) + bias_one
    activated, gelu_slope = gelu_parts(pre_act)
    act_rows = activated.astype(bf16)

    grad_out = cot_all.astype(f32)
    grad_mlp = (gate_mlp * grad_out).astype(bf16)
    grad_pre = (dot_nn(grad_mlp, wfc2_t) * gelu_slope).astype(bf16)
    cut = 512
    fc2_a_near = weight_term(grad_mlp, act_rows[:, :cut], f32)
    fc2_a_far = weight_term(grad_mlp, act_rows[:, n_fc2 : n_fc2 + cut], bf16)
    fc2_b_near = weight_term(grad_mlp, act_rows[:, cut:n_fc2], f32)
    fc2_b_far = weight_term(grad_mlp, act_rows[:, n_fc2 + cut :], f32)
    fc2_a_got = y_first_send(fc2_a_far)
    fc2_b_near, fc2_b_far, fc2_b_got = x_first_send(fc2_b_near, fc2_b_far)
    mlp_part = dot_nt(act_rows, wfc2_t)
    grad_mlp_part = dot_nt(grad_pre, wfc1)
    mlp_out = sum_cores_own(mlp_part) + b_fc2.astype(f32)
    result = middle[:tok_rows] + gate_mlp * mlp_out
    d_gate_mlp = grad_out[:tok_rows] * mlp_out
    fc1_a_far = weight_term(mlp_in, grad_pre[:, n_fc1 : n_fc1 + cut], bf16)
    fc1_a_near = weight_term(mlp_in, grad_pre[:, :cut], f32)
    fc1_b_near = weight_term(mlp_in, grad_pre[:, cut:n_fc1], f32)
    fc1_b_far = weight_term(mlp_in, grad_pre[:, n_fc1 + cut :], f32)
    fc2_a_got = after(fc2_a_got, fc1_b_far, fc1_a_near)
    fc2_b_got = after(fc2_b_got, fc1_b_far, fc1_a_near)
    fc2_a_keep, fc2_a_got = y_first_mid(fc2_a_near, fc2_a_got)
    fc2_b_keep, fc2_b_got = x_first_mid(fc2_b_near, fc2_b_far, fc2_b_got)
    fc1_a_got = y_first_send(fc1_a_far)
    fc1_b_near, fc1_b_far, fc1_b_got = x_first_send(fc1_b_near, fc1_b_far)
    grad_mlp_in = sum_cores_all(grad_mlp_part)
    d_scale_mlp = grad_mlp_in * normed_two
    grad_middle = grad_out + norm_back(normed_two, inverse_two, grad_mlp_in * (1.0 + scale_mlp))

    grad_attn = (gate_attn * grad_middle).astype(bf16)
    d_gate_attn = grad_middle * attn_out
    grad_mix = dot_nn(grad_attn, wproj_t).astype(bf16)
    proj_far = weight_term(grad_attn, mix_rows[:, n_proj:], bf16)
    proj_near = weight_term(grad_attn, mix_rows[:, :n_proj], f32)
    lse_rows = lse.T.reshape(heads, 1, 2 * tok_rows)
    fc2_a_got = after(fc2_a_got, grad_mix, proj_near)
    fc2_b_got = after(fc2_b_got, grad_mix, proj_near)
    fc2_sum = jnp.concatenate(
        [fc2_a_keep + fc2_a_got.astype(f32), fc2_b_keep + fc2_b_got.astype(f32)], axis=2
    )
    grad_far = attend_back(qkv, grad_mix, lse_rows, heads // 2, heads // 2)
    qkv_far = weight_term(attn_in, grad_far, bf16)
    fc1_a_got = after(fc1_a_got, grad_far)
    fc1_b_got = after(fc1_b_got, grad_far)
    fc1_a_keep, fc1_a_got = y_first_mid(fc1_a_near, fc1_a_got)
    fc1_b_keep, fc1_b_got = x_first_mid(fc1_b_near, fc1_b_far, fc1_b_got)
    proj_got = y_first_send(proj_far)
    qkv_got = y_first_send(qkv_far)
    grad_near = attend_back(qkv, after(grad_mix, grad_far), lse_rows, 0, heads // 2)
    proj_got = after(proj_got, grad_near)
    qkv_near = weight_term(attn_in, grad_near, f32)
    owned_fc2 = low_stages(fc2_sum, [grad_far, grad_near]).T
    fc1_a_got = after(fc1_a_got, grad_near)
    fc1_b_got = after(fc1_b_got, grad_near)
    fc1_sum = jnp.concatenate(
        [fc1_a_keep + fc1_a_got.astype(f32), fc1_b_keep + fc1_b_got.astype(f32)], axis=2
    )
    grad_attn_part = dot_nt(grad_near, wqkv[:, :n_qkv]) + dot_nt(grad_far, wqkv[:, n_qkv:])
    qkv_keep, qkv_got = y_first_mid(qkv_near, qkv_got)
    proj_keep, proj_got = y_first_mid(proj_near, proj_got)
    owned_fc1 = low_stages(fc1_sum, [grad_attn_part])
    grad_attn_in = sum_cores_own(grad_attn_part)
    d_scale_attn = grad_attn_in * normed_one[:tok_rows]
    grad_tokens = grad_middle[:tok_rows] + norm_back(
        normed_one[:tok_rows], inverse_one[:tok_rows], grad_attn_in * (1.0 + scale_attn)
    )
    owned_qkv = low_stages(qkv_keep + qkv_got.astype(f32), [])
    owned_proj = low_stages(proj_keep + proj_got.astype(f32), []).T

    own = [
        jnp.sum(term[:tok_rows], axis=0)
        for term in (grad_attn_in, d_scale_attn, d_gate_attn, grad_mlp_in, d_scale_mlp, d_gate_mlp)
    ]
    mod_sums = jnp.concatenate(own)
    mod_sums = mod_sums + swap_cores(mod_sums)
    by_rank = mod_sums.reshape(4, ada_cols)
    mod_keep = lax.dynamic_index_in_dim(by_rank, t_at, 0, False)
    mod_send = lax.dynamic_index_in_dim(by_rank, t_at ^ 2, 0, False)

    def value_sums(grads):
        sums = jnp.sum(grads.astype(f32), axis=0).reshape(heads // 2, 3, head_size)
        return jnp.concatenate([sums[:, :1], sums[:, 2:]], axis=1).reshape(n_bqv)

    b1_sums = jnp.sum(grad_pre.astype(f32), axis=0)
    bias_near = jnp.concatenate([value_sums(grad_near), b1_sums[:n_fc1]])
    bias_far = jnp.concatenate([value_sums(grad_far), b1_sums[n_fc1:]])
    out_sums = jnp.concatenate(
        [jnp.sum(grad_attn.astype(f32), axis=0), jnp.sum(grad_mlp.astype(f32), axis=0)]
    )
    got = swap_y(jnp.concatenate([mod_send, bias_far, out_sums]))
    mod_got, rest = got[:ada_cols], got[ada_cols:]
    sums = jnp.concatenate([bias_near, out_sums]) + rest
    grad_mod = ordered(y_at, mod_keep[None], mod_got[None], 0)
    for bit in range(dp_bits()):
        size = grad_mod.size
        got = swap_dp(jnp.concatenate([grad_mod.reshape(size), sums]), bit)
        grad_mod = ordered(own_bit(bit), grad_mod, got[:size].reshape(grad_mod.shape), 0)
        sums = sums + got[size:]
    owned_ada = lax.dot_general(
        silu_mine.astype(f32), grad_mod, (((0,), (0,)), ((), ())), precision=highest
    )
    grad_ba = jnp.sum(grad_mod, axis=0)
    silu_part = lax.dot_general(
        grad_mod, w_ada.astype(f32), (((1,), (1,)), ((), ())), precision=highest
    )
    silu_part = silu_part + swap_cores(silu_part)
    silu_part = silu_part + swap_y(silu_part)
    latents = condition.shape[0]
    grad_silu = exchange_small(silu_part.reshape(dp_size, latents, ada_rows))
    cond_vals = condition.astype(f32)
    cond_sigmoid = jax.nn.sigmoid(cond_vals)
    grad_condition = grad_silu * cond_sigmoid * (1.0 + cond_vals * (1.0 - cond_sigmoid))
    n_bias = n_bqv + n_fc1
    return (
        result.astype(bf16),
        grad_tokens,
        grad_condition,
        owned_ada,
        grad_ba,
        owned_qkv,
        sums[:n_bqv],
        owned_proj,
        sums[n_bias : n_bias + width],
        owned_fc1,
        sums[n_bqv:n_bias],
        owned_fc2,
        sums[n_bias + width :],
    )


def solution(mesh):
    placed = (
        P(("dp", "tensor"), None),
        P("dp", None),
        P("dp", "tensor"),
        P("tensor"),
        P("dp", "tensor"),
        P("tensor"),
        P("tensor", "dp"),
        P(),
        P("dp", "tensor"),
        P("tensor"),
        P("tensor", "dp"),
        P(),
        P(("dp", "tensor"), None),
    )
    return jax.shard_map(
        shards,
        mesh=mesh,
        in_specs=placed,
        out_specs=(
            P(("dp", "tensor"), None),
            P(("dp", "tensor"), None),
            P("dp", None),
            P("dp", "tensor"),
            P("tensor"),
            P("dp", "tensor"),
            P("tensor"),
            P("tensor", "dp"),
            P(),
            P("dp", "tensor"),
            P("tensor"),
            P("tensor", "dp"),
            P(),
        ),
        check_vma=False,
    )
```

```python
import jax
import jax.numpy as jnp
from jax import lax
from jax.experimental import pallas as pl
from jax.experimental.pallas import tpu as pltpu
from jax.sharding import PartitionSpec as P

HEAD_DIM = 72
SEQ = 1024

highest = lax.Precision.HIGHEST
root_two_pi = 0.7978845608028654
cubic_term = 0.044715
epsilon = 1e-06
log2_e = 1.4426950408889634
bf16 = jnp.bfloat16
f32 = jnp.float32


def swap_cores(values):
    return lax.ppermute(values, "tensor", [(i, i ^ 1) for i in range(4)])


def swap_y(values):
    return lax.ppermute(values, "tensor", [(i, i ^ 2) for i in range(4)])


def swap_apart(values, apart):
    size = lax.axis_size("dp")
    return lax.ppermute(values, "dp", [(i, i ^ apart) for i in range(size)])


def swap_dp(values, bit):
    return swap_apart(values, 1 << bit)


def swap_diagonal(values):
    size = 4 * lax.axis_size("dp")
    return lax.ppermute(values, ("dp", "tensor"), [(i, i ^ 6) for i in range(size)])


def after(values, *deps):
    return lax.optimization_barrier((values, deps))[0]


def dp_bits():
    return lax.axis_size("dp").bit_length() - 1


def own_bit(bit):
    return (lax.axis_index("dp") >> bit) & 1


def ordered(flag, mine, theirs, axis):
    first = jnp.where(flag == 0, mine, theirs)
    second = jnp.where(flag == 0, theirs, mine)
    return jnp.concatenate([first, second], axis=axis)


def gather_small(values):
    for bit in range(dp_bits()):
        values = ordered(own_bit(bit), values, swap_dp(values, bit), 0)
    return values


def scatter_small(values):
    for bit in reversed(range(dp_bits())):
        halves = values.reshape((2, values.shape[0] // 2) + values.shape[1:])
        mine = own_bit(bit)
        keep = lax.dynamic_index_in_dim(halves, mine, 0, False)
        send = lax.dynamic_index_in_dim(halves, 1 - mine, 0, False)
        values = keep + swap_dp(send, bit)
    return values


def exchange_small(values):
    dp, k, n = values.shape
    values = values[:, :, None]
    for bit in range(dp_bits()):
        pairs = values.reshape((values.shape[0] // 2, 2) + values.shape[1:])
        mine = own_bit(bit)
        keep = lax.dynamic_index_in_dim(pairs, mine, 1, False)
        send = lax.dynamic_index_in_dim(pairs, 1 - mine, 1, False)
        values = ordered(mine, keep, swap_dp(send, bit), 2)
    return values.reshape(k, dp * n)


def width_of(weight):
    return weight[2] - weight[1]


def height_of(weight):
    return sum(piece.shape[0] for piece in weight[0])


def row_step(
    body, rows, block, row_inputs, flat_inputs, weights, row_outputs, sum_outputs, name, flops=0
):
    steps = rows // block
    arrays, specs = [], []
    for entry in row_inputs:
        array, index = entry if isinstance(entry, tuple) else (entry, lambda i: i)
        arrays.append(array)
        specs.append(pl.BlockSpec((block, array.shape[1]), lambda i, index=index: (index(i), 0)))
    for array in flat_inputs:
        arrays.append(array)
        specs.append(pl.BlockSpec(array.shape, lambda i, nd=array.ndim: (0,) * nd))
    spans = [
        (lo // 128 * 128, min(-(-hi // 128) * 128, pieces[0].shape[1])) for pieces, lo, hi in weights
    ]
    counts = [len(pieces) for pieces, _, _ in weights]
    for pieces, _, _ in weights:
        arrays += pieces
        specs += [pl.BlockSpec(memory_space=pl.ANY)] * len(pieces)
    outs, out_specs = [], []
    for columns, kind in row_outputs:
        outs.append(jax.ShapeDtypeStruct((rows, columns), kind))
        out_specs.append(pl.BlockSpec((block, columns), lambda i: (i, 0)))
    for count, columns in sum_outputs:
        outs.append(jax.ShapeDtypeStruct((count, columns), f32))
        out_specs.append(pl.BlockSpec((count, columns), lambda i: (0, 0)))
    scratch = []
    for weight, (lo, hi) in zip(weights, spans):
        scratch += [pltpu.VMEM((height_of(weight), hi - lo), bf16), pltpu.SemaphoreType.DMA((len(weight[0]),))]
    n_row, n_flat = len(row_inputs), len(flat_inputs)

    def kernel(*refs):
        refs = list(refs)

        def take(count):
            part = refs[:count]
            del refs[:count]
            return part

        row_refs, flat_refs = take(n_row), take(n_flat)
        weight_refs = [take(count) for count in counts]
        out_refs, sum_refs = take(len(row_outputs)), take(len(sum_outputs))
        targets = [take(2) for _ in weights]
        step = pl.program_id(0)

        @pl.when(step == 0)
        def _():
            copies = []
            for refs, (target, sems), (lo, hi) in zip(weight_refs, targets, spans):
                at = 0
                for i, ref in enumerate(refs):
                    rows = ref.shape[0]
                    copies.append(
                        pltpu.make_async_copy(
                            ref.at[:, lo:hi], target.at[at : at + rows], sems.at[i]
                        )
                    )
                    at += rows
            for copy in copies:
                copy.start()
            for ref in sum_refs:
                ref[...] = jnp.zeros_like(ref)
            for copy in copies:
                copy.wait()

        views = [
            target.at[:, lo - at : hi - at]
            for (target, _), (_, lo, hi), (at, _) in zip(targets, weights, spans)
        ]
        body(step, row_refs, flat_refs, views, out_refs, sum_refs)

    moved = sum(a.size * a.dtype.itemsize for a in arrays) + sum(
        o.size * o.dtype.itemsize for o in outs
    )
    return pl.pallas_call(
        kernel,
        out_shape=outs,
        grid=(steps,),
        in_specs=specs,
        out_specs=out_specs,
        scratch_shapes=scratch,
        compiler_params=pltpu.CompilerParams(vmem_limit_bytes=58 << 20),
        cost_estimate=pl.CostEstimate(flops=flops, transcendentals=0, bytes_accessed=moved),
        name=name,
    )(*arrays)


def dot_nt(left_rows, right_mat):
    return lax.dot_general(
        left_rows, right_mat, (((1,), (1,)), ((), ())), preferred_element_type=f32
    )


def dot_nn(left_rows, right_mat):
    return jnp.dot(left_rows, right_mat, preferred_element_type=f32)


def normed_of(values):
    centre = values - jnp.mean(values, axis=-1, keepdims=True)
    inverse = lax.rsqrt(jnp.mean(centre * centre, axis=-1, keepdims=True) + epsilon)
    return centre * inverse, inverse


def norm_back(normed, inverse, grad_in):
    mean_grad = jnp.mean(grad_in, axis=-1, keepdims=True)
    mean_cross = jnp.mean(grad_in * normed, axis=-1, keepdims=True)
    return inverse * (grad_in - mean_grad - normed * mean_cross)


def rows_sum(values):
    return jnp.sum(values, axis=0, keepdims=True)


def norm_project(tokens, scale, shift, bias, weight):
    rows, width = tokens.shape
    n = width_of(weight)

    def body(step, ins, flat, w, outs, sums):
        normed, _ = normed_of(ins[0][...].astype(f32))
        attn_in = (normed * (1.0 + flat[0][...]) + flat[1][...]).astype(bf16)
        outs[0][...] = attn_in
        outs[1][...] = (dot_nn(attn_in, w[0][...]) + flat[2][...]).astype(bf16)

    return row_step(
        body, rows, 256, [tokens], [scale, shift, bias], [weight],
        [(width, bf16), (n, bf16)], [], "norm_project",
    )


def project(values, bias, weight):
    n = width_of(weight)

    def body(step, ins, flat, w, outs, sums):
        outs[0][...] = (dot_nn(ins[0][...], w[0][...]) + flat[0][...]).astype(bf16)

    return row_step(body, values.shape[0], 256, [values], [bias], [weight], [(n, bf16)], [], "project")[0]


def project_out(mix_near, mix_far, near, far):
    def body(step, ins, flat, w, outs, sums):
        total = dot_nt(ins[0][...], w[0][...]) + dot_nt(ins[1][...], w[1][...])
        outs[0][...] = total.astype(bf16)

    width = height_of(near)
    rows = mix_near.shape[0]
    return row_step(
        body, rows, 256, [mix_near, mix_far], [], [near, far], [(width, bf16)], [], "project_out"
    )[0]


def other_half(steps):
    return lambda i: jnp.where(i < steps // 2, i + steps // 2, i - steps // 2)


def middle_norm(mine, theirs, tokens, cotangent, b_proj, gate_attn, scale_mlp, shift_mlp, gate_mlp):
    rows, width = tokens.shape
    block = 256

    def body(step, ins, flat, w, outs, sums):
        attn_out = ins[0][...].astype(f32) + ins[1][...].astype(f32) + flat[0][...]
        middle = ins[2][...].astype(f32) + flat[1][...] * attn_out
        outs[0][...] = middle
        normed, _ = normed_of(middle)
        outs[1][...] = (normed * (1.0 + flat[2][...]) + flat[3][...]).astype(bf16)
        grad_mlp = (flat[4][...] * ins[3][...].astype(f32)).astype(bf16)
        outs[2][...] = grad_mlp
        sums[0][...] += rows_sum(grad_mlp.astype(f32))

    return row_step(
        body, rows, block, [mine, (theirs, other_half(rows // block)), tokens, cotangent],
        [b_proj, gate_attn, scale_mlp, shift_mlp, gate_mlp], [],
        [(width, f32), (width, bf16), (width, bf16)], [(1, width)], "middle_norm",
    )


def gelu_parts(pre_act):
    tangent = jnp.tanh(root_two_pi * (pre_act + cubic_term * pre_act * pre_act * pre_act))
    activated = 0.5 * pre_act * (1.0 + tangent)
    gelu_slope = 0.5 * (1.0 + tangent) + 0.5 * pre_act * (1.0 - tangent * tangent) * root_two_pi * (
        1.0 + 3.0 * cubic_term * pre_act * pre_act
    )
    return activated, gelu_slope


def feed_forward(mlp_in, bias, weight):
    n = width_of(weight)

    def body(step, ins, flat, w, outs, sums):
        activated, slope = gelu_parts(dot_nn(ins[0][...], w[0][...]) + flat[0][...])
        outs[0][...] = activated.astype(bf16)
        outs[1][...] = slope

    return row_step(
        body, mlp_in.shape[0], 256, [mlp_in], [bias], [weight], [(n, bf16), (n, f32)], [], "feed_forward"
    )


def feed_back(grad_mlp, act, slope, added, fc1, fc2, kind):
    rows, width = grad_mlp.shape
    n = act.shape[1]

    def body(step, ins, flat, w, outs, sums):
        grad_pre = (dot_nn(ins[0][...], w[1][...]) * ins[2][...]).astype(bf16)
        outs[0][...] = grad_pre
        sums[0][...] += rows_sum(grad_pre.astype(f32))
        grad_in = dot_nt(grad_pre, w[0][...])
        out = dot_nt(ins[1][...], w[1][...])
        if added is not None:
            grad_in = grad_in + ins[3][...]
            out = out + ins[4][...]
        outs[1][...] = grad_in.astype(kind)
        outs[2][...] = out.astype(kind)

    return row_step(
        body, rows, 256, [grad_mlp, act, slope] + ([] if added is None else list(added)), [], [fc1, fc2],
        [(n, bf16), (width, kind), (width, kind)], [(1, n)], "feed_back",
    )


def middle_back(
    grad_mine, grad_theirs, middle, cotangent, mine, theirs, b_proj, gate_attn, scale_mlp, near, far
):
    rows, width = middle.shape
    block = 256
    steps = rows // block
    n = width_of(near)

    def body(step, ins, flat, w, outs, sums):
        grad_in = ins[0][...].astype(f32) + ins[1][...].astype(f32)
        normed, inverse = normed_of(ins[2][...])
        grad_middle = ins[3][...].astype(f32) + norm_back(
            normed, inverse, grad_in * (1.0 + flat[2][...])
        )
        outs[0][...] = grad_middle
        grad_attn = (flat[1][...] * grad_middle).astype(bf16)
        outs[1][...] = grad_attn
        outs[2][...] = dot_nn(grad_attn, w[0][...]).astype(bf16)
        outs[3][...] = dot_nn(grad_attn, w[1][...]).astype(bf16)
        sums[0][3:4] += rows_sum(grad_attn.astype(f32))

        @pl.when(step < steps // 2)
        def _():
            attn_out = ins[4][...].astype(f32) + ins[5][...].astype(f32) + flat[0][...]
            sums[0][0:1] += rows_sum(grad_in)
            sums[0][1:2] += rows_sum(grad_in * normed)
            sums[0][2:3] += rows_sum(grad_middle * attn_out)

    flip = other_half(steps)
    return row_step(
        body, rows, block,
        [grad_mine, (grad_theirs, flip), middle, cotangent, mine, (theirs, flip)],
        [b_proj, gate_attn, scale_mlp], [near, far],
        [(width, f32), (width, bf16), (n, bf16), (n, bf16)], [(8, width)], "middle_back",
    )


def project_back(grads, weight, added, kind):
    width = height_of(weight)

    def body(step, ins, flat, w, outs, sums):
        total = dot_nt(ins[0][...], w[0][...])
        if added is not None:
            total = total + ins[1][...]
        outs[0][...] = total.astype(kind)

    inputs = [grads] if added is None else [grads, added]
    return row_step(
        body, grads.shape[0], 256, inputs, [], [weight], [(width, kind)], [], "project_back"
    )[0]


def first_back(mine, theirs, tokens, grad_middle, scale_attn):
    rows, width = tokens.shape

    def body(step, ins, flat, w, outs, sums):
        grad_in = ins[0][...].astype(f32) + ins[1][...].astype(f32)
        normed, inverse = normed_of(ins[2][...].astype(f32))
        outs[0][...] = ins[3][...] + norm_back(normed, inverse, grad_in * (1.0 + flat[0][...]))
        sums[0][0:1] += rows_sum(grad_in)
        sums[0][1:2] += rows_sum(grad_in * normed)

    return row_step(
        body, rows, 256, [mine, theirs, tokens, grad_middle], [scale_attn], [],
        [(width, f32)], [(8, width)], "first_back",
    )


def finish(mine, theirs, middle, cotangent, b_fc2, gate_mlp):
    rows, width = cotangent.shape

    def body(step, ins, flat, w, outs, sums):
        mlp_out = ins[0][...].astype(f32) + ins[1][...].astype(f32) + flat[0][...]
        outs[0][...] = (ins[2][...] + flat[1][...] * mlp_out).astype(bf16)
        sums[0][...] += rows_sum(ins[3][...].astype(f32) * mlp_out)

    return row_step(
        body, rows, 256, [mine, theirs, middle, cotangent], [b_fc2, gate_mlp], [],
        [(width, bf16)], [(1, width)], "finish",
    )


def gather_start(shard):
    half = lax.axis_size("dp") // 2
    if half <= 4:
        return [shard] + [swap_apart(shard, 2 * r) for r in range(1, half)]
    blocks = shard[None]
    for bit in range(1, dp_bits()):
        blocks = jnp.concatenate([blocks, swap_dp(blocks, bit)], axis=0)
    return list(blocks)


def gather_end(mine, theirs):
    half, rows, n = mine.shape
    blocks = jnp.stack([mine, theirs], axis=1).reshape(2 * half, rows, n)
    for bit in range(dp_bits()):
        pairs = blocks.reshape(half >> bit, 2, 1 << bit, rows, n)
        blocks = jnp.where(own_bit(bit) == 0, pairs, pairs[:, ::-1]).reshape(blocks.shape)
    return blocks.reshape(2 * half * rows, n)


def split_bit(blocks, axis, bit):
    mine = own_bit(bit)
    keep = lax.dynamic_index_in_dim(blocks, mine, axis, False)
    send = lax.dynamic_index_in_dim(blocks, 1 - mine, axis, False)
    return keep, send.astype(bf16)


def weight_term(left, right, kind):
    out = lax.dot_general(left, right, (((0,), (0,)), ((), ())), preferred_element_type=f32)
    dp = lax.axis_size("dp")
    return out.astype(kind).reshape(dp // 2, 2, out.shape[0] // dp, out.shape[1])


def relay_first(far):
    keep, other = split_bit(far, 1, 0)
    half = other.shape[0] // 2
    return keep, other[:half], other[half:]


def relay_sends(near, far_keep, by_x, by_y):
    near_keep, near_other = split_bit(near, 1, 0)
    half = by_x.shape[0]
    to_x = jnp.concatenate([near_other[:half], near_other[half:] + by_y], axis=0)
    to_y = jnp.concatenate([far_keep[:half] + by_x, far_keep[half:]], axis=0)
    return near_keep, to_x, to_y


def scatter_z_sends(total):
    half = total.shape[0]
    if half > 4:
        for bit in range(dp_bits() - 1, 1, -1):
            blocks = total.reshape((2, total.shape[0] // 2) + total.shape[1:])
            keep, send = split_bit(blocks, 0, bit)
            total = keep + swap_dp(send, bit).astype(f32)
        keep, send = split_bit(total, 0, 1)
        return keep, [send]
    here = lax.axis_index("dp") >> 1
    sends = [
        lax.dynamic_index_in_dim(total, here ^ r, 0, False).astype(bf16) for r in range(1, half)
    ]
    return lax.dynamic_index_in_dim(total, here, 0, False), sends


def scatter_z(sends):
    return [swap_apart(send, 2 * (r + 1)) for r, send in enumerate(sends)]


def add_all(keep, got):
    for part in got:
        keep = keep + part.astype(f32)
    return keep


def attend(qkv, block=512, unroll=2):
    rows, cols = qkv.shape
    size = HEAD_DIM
    heads = cols // (3 * size)
    factor = size ** (-0.5) * log2_e

    def kernel(x_ref, mix_ref, lse_ref, q_s, k_s, v_s, o_s, l_s):
        i = pl.program_id(0)

        @pl.when(i == 0)
        def _():
            for h in range(heads):
                b = h * 3 * size
                q_s[h] = x_ref[:, b : b + size]
                k_s[h] = x_ref[:, b + size : b + 2 * size]
                v_s[h] = x_ref[:, b + 2 * size : b + 3 * size]

        def one(h):
            q = q_s[h, pl.ds(pl.multiple_of(i * block, block), block), :]
            scores = lax.dot_general(
                q, k_s[h], (((1,), (1,)), ((), ())), preferred_element_type=f32
            )
            top = jnp.max(scores, axis=-1, keepdims=True)
            probs = jnp.exp2((scores - top) * factor)
            total = jnp.sum(probs, axis=-1, keepdims=True)
            out = jnp.dot(probs.astype(bf16), v_s[h], preferred_element_type=f32)
            o_s[h] = (out / total).astype(bf16)
            l_s[h] = top * factor + jnp.log2(total)

        def body(g, _):
            for u in range(unroll):
                one(g * unroll + u)
            return 0

        lax.fori_loop(0, heads // unroll, body, 0)
        for h in range(heads):
            mix_ref[:, h * size : (h + 1) * size] = o_s[h]
            lse_ref[:, h : h + 1] = l_s[h]

    return pl.pallas_call(
        kernel,
        out_shape=(
            jax.ShapeDtypeStruct((rows, heads * size), bf16),
            jax.ShapeDtypeStruct((rows, heads), f32),
        ),
        grid=(rows // block,),
        in_specs=[pl.BlockSpec((rows, cols), lambda i: (0, 0))],
        out_specs=(
            pl.BlockSpec((block, heads * size), lambda i: (i, 0)),
            pl.BlockSpec((block, heads), lambda i: (i, 0)),
        ),
        scratch_shapes=[pltpu.VMEM((heads, rows, size), bf16)] * 3
        + [pltpu.VMEM((heads, block, size), bf16), pltpu.VMEM((heads, block, 1), f32)],
        compiler_params=pltpu.CompilerParams(vmem_limit_bytes=48 << 20),
        cost_estimate=pl.CostEstimate(
            flops=16 * heads * rows * rows * size,
            transcendentals=heads * rows * rows,
            bytes_accessed=rows * cols * 2 + rows * heads * size * 2,
        ),
        name="attend",
    )(qkv)


def attend_back(qkv, grad_mix, lse, first, heads, block=512, unroll=2):
    rows, cols = qkv.shape
    size = HEAD_DIM
    all_heads = cols // (3 * size)
    factor = size ** (-0.5) * log2_e
    scale = size ** (-0.5)
    steps = rows // block

    def kernel(x_ref, g_ref, lse_ref, out_ref, q_s, k_s, v_s, g_s, dq_s, dk_s, dv_s):
        i = pl.program_id(0)

        @pl.when(i == 0)
        def _():
            for h in range(heads):
                b = (first + h) * 3 * size
                q_s[h] = x_ref[:, b : b + size]
                k_s[h] = x_ref[:, b + size : b + 2 * size]
                v_s[h] = x_ref[:, b + 2 * size : b + 3 * size]
                g_s[h] = g_ref[:, (first + h) * size : (first + h + 1) * size]
            dk_s[...] = jnp.zeros_like(dk_s)
            dv_s[...] = jnp.zeros_like(dv_s)

        at = pl.ds(pl.multiple_of(i * block, block), block)

        def one(h):
            q = q_s[h, at, :]
            g = g_s[h, at, :]
            k = k_s[h]
            scores = lax.dot_general(k, q, (((1,), (1,)), ((), ())), preferred_element_type=f32)
            probs = jnp.exp2(scores * factor - lse_ref[first + h, :, at])
            grad_probs = lax.dot_general(
                v_s[h], g, (((1,), (1,)), ((), ())), preferred_element_type=f32
            )
            inner = jnp.sum(probs * grad_probs, axis=0, keepdims=True)
            grad_scores = (probs * (grad_probs - inner)).astype(bf16)
            dv_s[h] += jnp.dot(probs.astype(bf16), g, preferred_element_type=f32)
            dk_s[h] += jnp.dot(grad_scores, q, preferred_element_type=f32)
            grad_q = lax.dot_general(
                grad_scores, k, (((0,), (0,)), ((), ())), preferred_element_type=f32
            )
            dq_s[h, at, :] = (grad_q * scale).astype(bf16)

        def body(g, _):
            for u in range(unroll):
                one(g * unroll + u)
            return 0

        lax.fori_loop(0, heads // unroll, body, 0)

        @pl.when(i == steps - 1)
        def _():
            for h in range(heads):
                b = h * 3 * size
                out_ref[:, b : b + size] = dq_s[h]
                out_ref[:, b + size : b + 2 * size] = (dk_s[h] * scale).astype(bf16)
                out_ref[:, b + 2 * size : b + 3 * size] = dv_s[h].astype(bf16)

    return pl.pallas_call(
        kernel,
        out_shape=jax.ShapeDtypeStruct((rows, heads * 3 * size), bf16),
        grid=(steps,),
        in_specs=[
            pl.BlockSpec((rows, cols), lambda i: (0, 0)),
            pl.BlockSpec((rows, all_heads * size), lambda i: (0, 0)),
            pl.BlockSpec((all_heads, 1, rows), lambda i: (0, 0, 0)),
        ],
        out_specs=pl.BlockSpec((rows, heads * 3 * size), lambda i: (0, 0)),
        scratch_shapes=[pltpu.VMEM((heads, rows, size), bf16)] * 5
        + [pltpu.VMEM((heads, rows, size), f32)] * 2,
        compiler_params=pltpu.CompilerParams(vmem_limit_bytes=56 << 20),
        cost_estimate=pl.CostEstimate(
            flops=40 * heads * rows * rows * size,
            transcendentals=heads * rows * rows,
            bytes_accessed=rows * cols * 4,
        ),
        name="attend_back",
    )(qkv, grad_mix, lse)


def shards(
    tokens_in,
    condition,
    w_ada,
    b_ada,
    w_qkv,
    b_qv,
    w_proj,
    b_proj,
    w_fc1,
    b_fc1,
    w_fc2,
    b_fc2,
    cotangent,
):
    tok_rows, width = tokens_in.shape
    head_size = HEAD_DIM
    dp_at = lax.axis_index("dp")
    t_at = lax.axis_index("tensor")
    y_at = t_at // 2
    core_at = t_at % 2
    dp_size = lax.axis_size("dp")
    ada_rows, ada_cols = w_ada.shape
    n_qkv, n_proj, n_fc1, n_fc2 = w_qkv.shape[1], w_proj.shape[0], w_fc1.shape[1], w_fc2.shape[0]
    n_bqv = b_qv.shape[0]
    heads = n_qkv // (3 * head_size)

    latents = condition.shape[0]
    cond_all = gather_small(condition)

    gather = lambda shard: lax.all_gather(shard, "dp", axis=0, tiled=True)
    qkv_all = gather(jnp.pad(w_qkv, ((0, 0), (0, -n_qkv % 128))))
    fc1_all = gather(w_fc1)
    fc2_mine, proj_mine = w_fc2.T, w_proj.T
    theirs = swap_y(jnp.concatenate([fc2_mine, proj_mine], axis=1))
    fc2_all = gather(jnp.concatenate([fc2_mine, theirs[:, :n_fc2]], axis=1))
    proj_z = gather_start(jnp.concatenate([proj_mine, theirs[:, n_fc2:]], axis=1))
    qkv_theirs = swap_y(qkv_all)
    qkv_near, qkv_far = ((qkv_all,), 0, n_qkv), ((qkv_theirs,), 0, n_qkv)
    fc2_near, fc2_far = ((fc2_all,), 0, n_fc2), ((fc2_all,), n_fc2, 2 * n_fc2)
    fc1_theirs = swap_y(after(fc1_all, qkv_theirs))
    fc1_near, fc1_far = ((fc1_all,), 0, n_fc1), ((fc1_theirs,), 0, n_fc1)

    inputs_theirs = swap_cores(jnp.concatenate([tokens_in, cotangent], axis=0))
    tokens_all = jnp.concatenate([tokens_in, inputs_theirs[:tok_rows]], axis=0)
    cot_all = jnp.concatenate([cotangent, inputs_theirs[tok_rows:]], axis=0)

    cond_vals = cond_all.astype(f32)
    silu_all = (cond_vals * jax.nn.sigmoid(cond_vals)).astype(bf16)
    silu_mine = lax.dynamic_slice_in_dim(silu_all, dp_at * ada_rows, ada_rows, 1)
    mod_part = jnp.dot(silu_mine, w_ada, preferred_element_type=f32)
    mod_part = mod_part + jnp.where(dp_at == 0, b_ada.astype(f32), 0.0)
    by_y = mod_part.reshape(dp_size, 2, ada_cols)
    mod_keep = lax.dynamic_index_in_dim(by_y, y_at, 1, True)
    mod_send = lax.dynamic_index_in_dim(by_y, 1 - y_at, 1, False)
    bias_mine = jnp.concatenate([b_qv, b_fc1]).astype(f32)[None]
    mod_got = swap_y(jnp.concatenate([mod_send, bias_mine], axis=0))
    bias_theirs = mod_got[dp_size:]
    mod_two = ordered(y_at, mod_keep, mod_got[:dp_size, None], 1)
    mod_all = ordered(core_at, mod_two[:, :, None], swap_cores(mod_two)[:, :, None], 2)
    mod_all = mod_all.reshape(dp_size, 4 * ada_cols)
    for bit in range(dp_bits()):
        pairs = mod_all.reshape(mod_all.shape[0] // 2, 2, 4 * ada_cols)
        keep = lax.dynamic_index_in_dim(pairs, own_bit(bit), 1, False)
        send = lax.dynamic_index_in_dim(pairs, 1 - own_bit(bit), 1, False)
        mod_all = keep + swap_dp(send, bit)
    mod_row = after(mod_all, tokens_all, cot_all)

    shift_attn, scale_attn, gate_attn, shift_mlp, scale_mlp, gate_mlp = jnp.split(mod_row, 6, axis=1)

    def qkv_bias(values):
        pair = values[0, :n_bqv].reshape(heads, 2, head_size)
        return jnp.stack([pair[:, 0], jnp.zeros_like(pair[:, 0]), pair[:, 1]], axis=1).reshape(1, n_qkv)

    attn_in, qkv_n = norm_project(tokens_all, scale_attn, shift_attn, qkv_bias(bias_mine), qkv_near)
    mix_n, lse_n = attend(qkv_n)
    proj_own = jnp.stack(after(proj_z, mix_n))
    proj_theirs = swap_dp(proj_own, 0)
    qkv_f = project(after(attn_in, mix_n, proj_own), qkv_bias(bias_theirs), qkv_far)
    mix_f, lse_f = attend(qkv_f)
    proj_all = gather_end(proj_own, after(proj_theirs, mix_f))
    proj_near, proj_far = ((proj_all,), 0, n_proj), ((proj_all,), n_proj, 2 * n_proj)
    proj_row = b_proj.astype(f32)[None]
    out_mine = project_out(mix_n, mix_f, proj_near, proj_far)
    out_theirs = swap_cores(out_mine)
    middle, mlp_in, grad_mlp, grad_b2 = middle_norm(
        out_mine, out_theirs, tokens_all, cot_all, proj_row,
        gate_attn, scale_mlp, shift_mlp, gate_mlp,
    )

    act_n, slope_n = feed_forward(mlp_in, bias_mine[:, n_bqv:], fc1_near)
    act_f, slope_f = feed_forward(after(mlp_in, act_n), bias_theirs[:, n_bqv:], fc1_far)

    fc2_term_f = weight_term(grad_mlp, act_f, bf16)
    fc2_far_keep, *sends = relay_first(fc2_term_f)
    by_x, by_y = swap_dp(sends[0], 0), swap_y(sends[1])
    fc2_term_n = weight_term(grad_mlp, act_n, f32)
    pre_n, grad_in_near, mlp_near, b1_n = feed_back(
        after(grad_mlp, fc2_term_n, fc2_far_keep, sends), act_n, slope_n, None, fc1_near, fc2_near, f32
    )
    by_x, by_y = after((by_x, by_y), grad_in_near)
    fc2_keep, *sends = relay_sends(fc2_term_n, fc2_far_keep, by_x, by_y)
    fc2_got = swap_dp(sends[0], 0), swap_y(sends[1])
    pre_f, grad_in_mine, mlp_part, b1_f = feed_back(
        after(grad_mlp, sends), act_f, slope_f, (grad_in_near, mlp_near), fc1_far, fc2_far, bf16
    )
    grad_in_theirs = swap_cores(grad_in_mine)
    fc1_term_f = weight_term(mlp_in, after(pre_f, grad_in_mine), bf16)
    fc1_far_keep, *sends = relay_first(fc1_term_f)
    by_x, by_y = swap_dp(sends[0], 0), swap_y(sends[1])
    fc1_term_n = weight_term(mlp_in, pre_n, f32)
    fc2_got = after(fc2_got, fc1_term_n)
    fc2_keep, z_sends = scatter_z_sends(add_all(fc2_keep, fc2_got))
    grad_middle, grad_attn, gmix_n, gmix_f, mid_sums = middle_back(
        after(grad_in_mine, fc1_term_n, fc1_far_keep, sends, z_sends), grad_in_theirs, middle, cot_all,
        out_mine, out_theirs, proj_row, gate_attn, scale_mlp, proj_near, proj_far,
    )
    fc2_got = scatter_z(z_sends)

    proj_term_f = weight_term(grad_attn, mix_f, bf16)
    proj_term_n = weight_term(grad_attn, mix_n, f32)
    by_x, by_y = after((by_x, by_y), proj_term_n, fc2_got)
    fc1_keep, *sends = relay_sends(fc1_term_n, fc1_far_keep, by_x, by_y)
    fc1_got = swap_dp(sends[0], 0), swap_y(sends[1])
    rows_of = lambda lse: lse.T.reshape(heads, 1, 2 * tok_rows)
    grad_f = attend_back(
        qkv_f, after(gmix_f, proj_term_f, proj_term_n, sends), rows_of(lse_f), 0, heads
    )
    one_term_f = jnp.concatenate([weight_term(attn_in, grad_f, bf16), proj_term_f], axis=3)
    one_far_keep, *sends = relay_first(one_term_f)
    by_x, by_y = swap_dp(sends[0], 0), swap_y(sends[1])
    part_f = project_back(after(grad_f, sends), qkv_far, None, f32)
    fc1_got = after(fc1_got, part_f)
    fc1_keep, z_sends = scatter_z_sends(add_all(fc1_keep, fc1_got))
    fc1_got = scatter_z(z_sends)
    grad_n = attend_back(
        qkv_n, after(gmix_n, part_f, one_far_keep, z_sends), rows_of(lse_n), 0, heads
    )
    attn_part = project_back(after(grad_n, by_x, by_y), qkv_near, part_f, bf16)
    attn_theirs = swap_cores(attn_part[tok_rows:])
    one_term_n = jnp.concatenate(
        [weight_term(after(attn_in, attn_part, fc1_got), grad_n, f32), proj_term_n], axis=3
    )
    one_keep, *sends = relay_sends(one_term_n, one_far_keep, by_x, by_y)
    one_got = swap_dp(sends[0], 0), swap_y(sends[1])
    grad_tokens, one_sums = first_back(
        after(attn_part, sends), attn_theirs, tokens_in, grad_middle, scale_attn
    )
    mlp_theirs = swap_cores(after(mlp_part[tok_rows:], grad_n))
    result, gate_sums = finish(mlp_part, mlp_theirs, middle, cotangent, b_fc2.astype(f32)[None], gate_mlp)

    def value_sums(grads):
        sums = jnp.sum(grads.astype(f32), axis=0).reshape(heads, 3, head_size)
        return jnp.concatenate([sums[:, :1], sums[:, 2:]], axis=1).reshape(n_bqv)

    mod_sums = jnp.concatenate([one_sums[:2].reshape(-1), mid_sums[2], mid_sums[0], mid_sums[1], gate_sums[0]])
    mod_sums = mod_sums + swap_cores(mod_sums)
    sums = jnp.concatenate(
        [value_sums(grad_n), b1_n[0], mid_sums[3], grad_b2[0], value_sums(grad_f), b1_f[0]]
    )
    grad_mod = mod_sums[None]
    for bit in list(range(1, dp_bits())) + [0]:
        size = grad_mod.size
        if bit == 1:
            grad_mod = after(grad_mod, one_got)
        if bit == 0:
            one_keep, one_sends = scatter_z_sends(add_all(one_keep, after(one_got, grad_mod)))
            grad_mod = after(grad_mod, one_sends)
        got = swap_dp(jnp.concatenate([grad_mod.reshape(size), sums]), bit)
        theirs = got[:size].reshape(grad_mod.shape)
        if bit == 0:
            both = jnp.where(own_bit(0) == 0, jnp.stack([grad_mod, theirs], 1), jnp.stack([theirs, grad_mod], 1))
            grad_mod = both.reshape(dp_size, 4, ada_cols)
        else:
            grad_mod = ordered(own_bit(bit), grad_mod, theirs, 0)
        sums = sums + got[size:]
    mod_keep = lax.dynamic_index_in_dim(grad_mod, t_at, 1, False)
    mod_send = lax.dynamic_index_in_dim(grad_mod, t_at ^ 2, 1, False)
    n_bias = n_bqv + n_fc1
    shared = n_bias + 2 * width
    got = swap_y(jnp.concatenate([mod_send.reshape(-1), sums[n_bias:shared], sums[shared:]]))
    mod_got, rest = got[: mod_send.size].reshape(mod_send.shape), got[mod_send.size :]
    bias_sums = sums[:n_bias] + rest[2 * width :]
    out_sums = sums[n_bias:shared] + rest[: 2 * width]
    grad_mod = ordered(y_at, mod_keep[:, None], mod_got[:, None], 1).reshape(2 * dp_size, ada_cols)
    one_got = scatter_z(one_sends)
    owned_ada = lax.dot_general(
        silu_mine.astype(f32), after(grad_mod, one_sends), (((0,), (0,)), ((), ())), precision=highest
    )
    grad_ba = jnp.sum(grad_mod, axis=0)
    silu_part = lax.dot_general(
        after(grad_mod, one_sends), w_ada.astype(f32), (((1,), (1,)), ((), ())), precision=highest
    )
    silu_part = silu_part + swap_cores(silu_part)
    silu_part = silu_part + swap_y(silu_part)
    owned_one = add_all(one_keep, one_got)
    grad_silu = exchange_small(silu_part.reshape(dp_size, latents, ada_rows))
    cond_vals = condition.astype(f32)
    cond_sigmoid = jax.nn.sigmoid(cond_vals)
    grad_condition = grad_silu * cond_sigmoid * (1.0 + cond_vals * (1.0 - cond_sigmoid))
    return (
        result,
        grad_tokens,
        grad_condition,
        owned_ada,
        grad_ba,
        owned_one[:, :n_qkv],
        bias_sums[:n_bqv],
        owned_one[:, n_qkv:].T,
        out_sums[:width],
        add_all(fc1_keep, fc1_got),
        bias_sums[n_bqv:],
        add_all(fc2_keep, fc2_got).T,
        out_sums[width:],
    )


def solution(mesh):
    placed = (
        P(("dp", "tensor"), None),
        P("dp", None),
        P("dp", "tensor"),
        P("tensor"),
        P("dp", "tensor"),
        P("tensor"),
        P("tensor", "dp"),
        P(),
        P("dp", "tensor"),
        P("tensor"),
        P("tensor", "dp"),
        P(),
        P(("dp", "tensor"), None),
    )
    return jax.shard_map(
        shards,
        mesh=mesh,
        in_specs=placed,
        out_specs=(
            P(("dp", "tensor"), None),
            P(("dp", "tensor"), None),
            P("dp", None),
            P("dp", "tensor"),
            P("tensor"),
            P("dp", "tensor"),
            P("tensor"),
            P("tensor", "dp"),
            P(),
            P("dp", "tensor"),
            P("tensor"),
            P("tensor", "dp"),
            P(),
        ),
        check_vma=False,
    )
```

```python
import jax
import jax.numpy as jnp
from jax import lax
from jax.experimental import pallas as pl
from jax.experimental.pallas import tpu as pltpu
from jax.sharding import PartitionSpec as P

HEAD_DIM = 72
SEQ = 1024

highest = lax.Precision.HIGHEST
root_two_pi = 0.7978845608028654
cubic_term = 0.044715
epsilon = 1e-06
log2_e = 1.4426950408889634
bf16 = jnp.bfloat16
f32 = jnp.float32


def swap_cores(values):
    return lax.ppermute(values, "tensor", [(i, i ^ 1) for i in range(4)])


def swap_y(values):
    return lax.ppermute(values, "tensor", [(i, i ^ 2) for i in range(4)])


def swap_apart(values, apart):
    size = lax.axis_size("dp")
    return lax.ppermute(values, "dp", [(i, i ^ apart) for i in range(size)])


def swap_dp(values, bit):
    return swap_apart(values, 1 << bit)


def swap_diagonal(values):
    size = 4 * lax.axis_size("dp")
    return lax.ppermute(values, ("dp", "tensor"), [(i, i ^ 6) for i in range(size)])


def after(values, *deps):
    return lax.optimization_barrier((values, deps))[0]


def dp_bits():
    return lax.axis_size("dp").bit_length() - 1


def own_bit(bit):
    return (lax.axis_index("dp") >> bit) & 1


def ordered(flag, mine, theirs, axis):
    first = jnp.where(flag == 0, mine, theirs)
    second = jnp.where(flag == 0, theirs, mine)
    return jnp.concatenate([first, second], axis=axis)


def gather_small(values):
    for bit in range(dp_bits()):
        values = ordered(own_bit(bit), values, swap_dp(values, bit), 0)
    return values


def scatter_small(values):
    for bit in reversed(range(dp_bits())):
        halves = values.reshape((2, values.shape[0] // 2) + values.shape[1:])
        mine = own_bit(bit)
        keep = lax.dynamic_index_in_dim(halves, mine, 0, False)
        send = lax.dynamic_index_in_dim(halves, 1 - mine, 0, False)
        values = keep + swap_dp(send, bit)
    return values


def exchange_small(values):
    dp, k, n = values.shape
    values = values[:, :, None]
    for bit in range(dp_bits()):
        pairs = values.reshape((values.shape[0] // 2, 2) + values.shape[1:])
        mine = own_bit(bit)
        keep = lax.dynamic_index_in_dim(pairs, mine, 1, False)
        send = lax.dynamic_index_in_dim(pairs, 1 - mine, 1, False)
        values = ordered(mine, keep, swap_dp(send, bit), 2)
    return values.reshape(k, dp * n)


def width_of(weight):
    return weight[2] - weight[1]


def height_of(weight):
    return sum(piece.shape[0] for piece in weight[0])


def row_step(
    body, rows, block, row_inputs, flat_inputs, weights, row_outputs, sum_outputs, name, flops=0
):
    steps = rows // block
    arrays, specs = [], []
    for entry in row_inputs:
        array, index = entry if isinstance(entry, tuple) else (entry, lambda i: i)
        arrays.append(array)
        specs.append(pl.BlockSpec((block, array.shape[1]), lambda i, index=index: (index(i), 0)))
    for array in flat_inputs:
        arrays.append(array)
        specs.append(pl.BlockSpec(array.shape, lambda i, nd=array.ndim: (0,) * nd))
    spans = [
        (lo // 128 * 128, min(-(-hi // 128) * 128, pieces[0].shape[1])) for pieces, lo, hi in weights
    ]
    counts = [len(pieces) for pieces, _, _ in weights]
    for pieces, _, _ in weights:
        arrays += pieces
        specs += [pl.BlockSpec(memory_space=pl.ANY)] * len(pieces)
    outs, out_specs = [], []
    for columns, kind in row_outputs:
        outs.append(jax.ShapeDtypeStruct((rows, columns), kind))
        out_specs.append(pl.BlockSpec((block, columns), lambda i: (i, 0)))
    for count, columns in sum_outputs:
        outs.append(jax.ShapeDtypeStruct((count, columns), f32))
        out_specs.append(pl.BlockSpec((count, columns), lambda i: (0, 0)))
    scratch = []
    for weight, (lo, hi) in zip(weights, spans):
        scratch += [pltpu.VMEM((height_of(weight), hi - lo), bf16), pltpu.SemaphoreType.DMA((len(weight[0]),))]
    n_row, n_flat = len(row_inputs), len(flat_inputs)

    def kernel(*refs):
        refs = list(refs)

        def take(count):
            part = refs[:count]
            del refs[:count]
            return part

        row_refs, flat_refs = take(n_row), take(n_flat)
        weight_refs = [take(count) for count in counts]
        out_refs, sum_refs = take(len(row_outputs)), take(len(sum_outputs))
        targets = [take(2) for _ in weights]
        step = pl.program_id(0)

        @pl.when(step == 0)
        def _():
            copies = []
            for refs, (target, sems), (lo, hi) in zip(weight_refs, targets, spans):
                at = 0
                for i, ref in enumerate(refs):
                    rows = ref.shape[0]
                    copies.append(
                        pltpu.make_async_copy(
                            ref.at[:, lo:hi], target.at[at : at + rows], sems.at[i]
                        )
                    )
                    at += rows
            for copy in copies:
                copy.start()
            for ref in sum_refs:
                ref[...] = jnp.zeros_like(ref)
            for copy in copies:
                copy.wait()

        views = [
            target.at[:, lo - at : hi - at]
            for (target, _), (_, lo, hi), (at, _) in zip(targets, weights, spans)
        ]
        body(step, row_refs, flat_refs, views, out_refs, sum_refs)

    moved = sum(a.size * a.dtype.itemsize for a in arrays) + sum(
        o.size * o.dtype.itemsize for o in outs
    )
    return pl.pallas_call(
        kernel,
        out_shape=outs,
        grid=(steps,),
        in_specs=specs,
        out_specs=out_specs,
        scratch_shapes=scratch,
        compiler_params=pltpu.CompilerParams(vmem_limit_bytes=58 << 20),
        cost_estimate=pl.CostEstimate(flops=flops, transcendentals=0, bytes_accessed=moved),
        name=name,
    )(*arrays)


def dot_nt(left_rows, right_mat):
    return lax.dot_general(
        left_rows, right_mat, (((1,), (1,)), ((), ())), preferred_element_type=f32
    )


def dot_nn(left_rows, right_mat):
    return jnp.dot(left_rows, right_mat, preferred_element_type=f32)


def normed_of(values):
    centre = values - jnp.mean(values, axis=-1, keepdims=True)
    inverse = lax.rsqrt(jnp.mean(centre * centre, axis=-1, keepdims=True) + epsilon)
    return centre * inverse, inverse


def norm_back(normed, inverse, grad_in):
    mean_grad = jnp.mean(grad_in, axis=-1, keepdims=True)
    mean_cross = jnp.mean(grad_in * normed, axis=-1, keepdims=True)
    return inverse * (grad_in - mean_grad - normed * mean_cross)


def rows_sum(values):
    return jnp.sum(values, axis=0, keepdims=True)


def norm_project(tokens, scale, shift, bias, weight):
    rows, width = tokens.shape
    n = width_of(weight)

    def body(step, ins, flat, w, outs, sums):
        normed, _ = normed_of(ins[0][...].astype(f32))
        attn_in = (normed * (1.0 + flat[0][...]) + flat[1][...]).astype(bf16)
        outs[0][...] = attn_in
        outs[1][...] = (dot_nn(attn_in, w[0][...]) + flat[2][...]).astype(bf16)

    return row_step(
        body, rows, 256, [tokens], [scale, shift, bias], [weight],
        [(width, bf16), (n, bf16)], [], "norm_project",
    )


def project(values, bias, weight):
    n = width_of(weight)

    def body(step, ins, flat, w, outs, sums):
        outs[0][...] = (dot_nn(ins[0][...], w[0][...]) + flat[0][...]).astype(bf16)

    return row_step(body, values.shape[0], 256, [values], [bias], [weight], [(n, bf16)], [], "project")[0]


def project_out(mix_near, mix_far, near, far):
    def body(step, ins, flat, w, outs, sums):
        total = dot_nt(ins[0][...], w[0][...]) + dot_nt(ins[1][...], w[1][...])
        outs[0][...] = total.astype(bf16)

    width = height_of(near)
    rows = mix_near.shape[0]
    return row_step(
        body, rows, 256, [mix_near, mix_far], [], [near, far], [(width, bf16)], [], "project_out"
    )[0]


def other_half(steps):
    return lambda i: jnp.where(i < steps // 2, i + steps // 2, i - steps // 2)


def middle_norm(mine, theirs, tokens, cotangent, b_proj, gate_attn, scale_mlp, shift_mlp, gate_mlp):
    rows, width = tokens.shape
    block = 256

    def body(step, ins, flat, w, outs, sums):
        attn_out = ins[0][...].astype(f32) + ins[1][...].astype(f32) + flat[0][...]
        middle = ins[2][...].astype(f32) + flat[1][...] * attn_out
        outs[0][...] = middle
        normed, _ = normed_of(middle)
        outs[1][...] = (normed * (1.0 + flat[2][...]) + flat[3][...]).astype(bf16)
        grad_mlp = (flat[4][...] * ins[3][...].astype(f32)).astype(bf16)
        outs[2][...] = grad_mlp
        sums[0][...] += rows_sum(grad_mlp.astype(f32))

    return row_step(
        body, rows, block, [mine, (theirs, other_half(rows // block)), tokens, cotangent],
        [b_proj, gate_attn, scale_mlp, shift_mlp, gate_mlp], [],
        [(width, f32), (width, bf16), (width, bf16)], [(1, width)], "middle_norm",
    )


def gelu_parts(pre_act):
    tangent = jnp.tanh(root_two_pi * (pre_act + cubic_term * pre_act * pre_act * pre_act))
    activated = 0.5 * pre_act * (1.0 + tangent)
    gelu_slope = 0.5 * (1.0 + tangent) + 0.5 * pre_act * (1.0 - tangent * tangent) * root_two_pi * (
        1.0 + 3.0 * cubic_term * pre_act * pre_act
    )
    return activated, gelu_slope


def feed_forward(mlp_in, bias, weight):
    n = width_of(weight)

    def body(step, ins, flat, w, outs, sums):
        activated, slope = gelu_parts(dot_nn(ins[0][...], w[0][...]) + flat[0][...])
        outs[0][...] = activated.astype(bf16)
        outs[1][...] = slope

    return row_step(
        body, mlp_in.shape[0], 256, [mlp_in], [bias], [weight], [(n, bf16), (n, f32)], [], "feed_forward"
    )


def feed_back(grad_mlp, act, slope, added, fc1, fc2, kind):
    rows, width = grad_mlp.shape
    n = act.shape[1]

    def body(step, ins, flat, w, outs, sums):
        grad_pre = (dot_nn(ins[0][...], w[1][...]) * ins[2][...]).astype(bf16)
        outs[0][...] = grad_pre
        sums[0][...] += rows_sum(grad_pre.astype(f32))
        grad_in = dot_nt(grad_pre, w[0][...])
        out = dot_nt(ins[1][...], w[1][...])
        if added is not None:
            grad_in = grad_in + ins[3][...]
            out = out + ins[4][...]
        outs[1][...] = grad_in.astype(kind)
        outs[2][...] = out.astype(kind)

    return row_step(
        body, rows, 256, [grad_mlp, act, slope] + ([] if added is None else list(added)), [], [fc1, fc2],
        [(n, bf16), (width, kind), (width, kind)], [(1, n)], "feed_back",
    )


def middle_back(
    grad_mine, grad_theirs, middle, cotangent, mine, theirs, b_proj, gate_attn, scale_mlp, near, far
):
    rows, width = middle.shape
    block = 256
    steps = rows // block
    n = width_of(near)

    def body(step, ins, flat, w, outs, sums):
        grad_in = ins[0][...].astype(f32) + ins[1][...].astype(f32)
        normed, inverse = normed_of(ins[2][...])
        grad_middle = ins[3][...].astype(f32) + norm_back(
            normed, inverse, grad_in * (1.0 + flat[2][...])
        )
        outs[0][...] = grad_middle
        grad_attn = (flat[1][...] * grad_middle).astype(bf16)
        outs[1][...] = grad_attn
        outs[2][...] = dot_nn(grad_attn, w[0][...]).astype(bf16)
        outs[3][...] = dot_nn(grad_attn, w[1][...]).astype(bf16)
        sums[0][3:4] += rows_sum(grad_attn.astype(f32))

        @pl.when(step < steps // 2)
        def _():
            attn_out = ins[4][...].astype(f32) + ins[5][...].astype(f32) + flat[0][...]
            sums[0][0:1] += rows_sum(grad_in)
            sums[0][1:2] += rows_sum(grad_in * normed)
            sums[0][2:3] += rows_sum(grad_middle * attn_out)

    flip = other_half(steps)
    return row_step(
        body, rows, block,
        [grad_mine, (grad_theirs, flip), middle, cotangent, mine, (theirs, flip)],
        [b_proj, gate_attn, scale_mlp], [near, far],
        [(width, f32), (width, bf16), (n, bf16), (n, bf16)], [(8, width)], "middle_back",
    )


def project_back(grads, weight, added, kind):
    width = height_of(weight)

    def body(step, ins, flat, w, outs, sums):
        total = dot_nt(ins[0][...], w[0][...])
        if added is not None:
            total = total + ins[1][...]
        outs[0][...] = total.astype(kind)

    inputs = [grads] if added is None else [grads, added]
    return row_step(
        body, grads.shape[0], 256, inputs, [], [weight], [(width, kind)], [], "project_back"
    )[0]


def first_back(mine, theirs, tokens, grad_middle, scale_attn):
    rows, width = tokens.shape

    def body(step, ins, flat, w, outs, sums):
        grad_in = ins[0][...].astype(f32) + ins[1][...].astype(f32)
        normed, inverse = normed_of(ins[2][...].astype(f32))
        outs[0][...] = ins[3][...] + norm_back(normed, inverse, grad_in * (1.0 + flat[0][...]))
        sums[0][0:1] += rows_sum(grad_in)
        sums[0][1:2] += rows_sum(grad_in * normed)

    return row_step(
        body, rows, 256, [mine, theirs, tokens, grad_middle], [scale_attn], [],
        [(width, f32)], [(8, width)], "first_back",
    )


def finish(mine, theirs, middle, cotangent, b_fc2, gate_mlp):
    rows, width = cotangent.shape

    def body(step, ins, flat, w, outs, sums):
        mlp_out = ins[0][...].astype(f32) + ins[1][...].astype(f32) + flat[0][...]
        outs[0][...] = (ins[2][...] + flat[1][...] * mlp_out).astype(bf16)
        sums[0][...] += rows_sum(ins[3][...].astype(f32) * mlp_out)

    return row_step(
        body, rows, 256, [mine, theirs, middle, cotangent], [b_fc2, gate_mlp], [],
        [(width, bf16)], [(1, width)], "finish",
    )


def gather_start(shard):
    half = lax.axis_size("dp") // 2
    if half <= 4:
        return [shard] + [swap_apart(shard, 2 * r) for r in range(1, half)]
    blocks = shard[None]
    for bit in range(1, dp_bits()):
        blocks = jnp.concatenate([blocks, swap_dp(blocks, bit)], axis=0)
    return list(blocks)


def gather_end(mine, theirs):
    half, rows, n = mine.shape
    blocks = jnp.stack([mine, theirs], axis=1).reshape(2 * half, rows, n)
    for bit in range(dp_bits()):
        pairs = blocks.reshape(half >> bit, 2, 1 << bit, rows, n)
        blocks = jnp.where(own_bit(bit) == 0, pairs, pairs[:, ::-1]).reshape(blocks.shape)
    return blocks.reshape(2 * half * rows, n)


def split_bit(blocks, axis, bit):
    mine = own_bit(bit)
    keep = lax.dynamic_index_in_dim(blocks, mine, axis, False)
    send = lax.dynamic_index_in_dim(blocks, 1 - mine, axis, False)
    return keep, send.astype(bf16)


def weight_term(left, right, kind):
    out = lax.dot_general(left, right, (((0,), (0,)), ((), ())), preferred_element_type=f32)
    dp = lax.axis_size("dp")
    return out.astype(kind).reshape(dp // 2, 2, out.shape[0] // dp, out.shape[1])


def relay_first(far):
    keep, other = split_bit(far, 1, 0)
    half = other.shape[0] // 2
    return keep, other[:half], other[half:]


def relay_sends(near, far_keep, by_x, by_y):
    near_keep, near_other = split_bit(near, 1, 0)
    half = by_x.shape[0]
    to_x = jnp.concatenate([near_other[:half], near_other[half:] + by_y], axis=0)
    to_y = jnp.concatenate([far_keep[:half] + by_x, far_keep[half:]], axis=0)
    return near_keep, to_x, to_y


def scatter_z_sends(total):
    half = total.shape[0]
    if half > 4:
        for bit in range(dp_bits() - 1, 1, -1):
            blocks = total.reshape((2, total.shape[0] // 2) + total.shape[1:])
            keep, send = split_bit(blocks, 0, bit)
            total = keep + swap_dp(send, bit).astype(f32)
        keep, send = split_bit(total, 0, 1)
        return keep, [send]
    here = lax.axis_index("dp") >> 1
    sends = [
        lax.dynamic_index_in_dim(total, here ^ r, 0, False).astype(bf16) for r in range(1, half)
    ]
    return lax.dynamic_index_in_dim(total, here, 0, False), sends


def sum_and_split(keep, by_x, by_y):
    half, rows, n = keep.shape
    if half > 4:
        total = add_all(keep.astype(f32), (by_x, by_y))
        for bit in range(dp_bits() - 1, 1, -1):
            blocks = total.reshape((2, total.shape[0] // 2) + total.shape[1:])
            keep, send = split_bit(blocks, 0, bit)
            total = keep + swap_dp(send, bit).astype(f32)
        keep, send = split_bit(total, 0, 1)
        return keep, [send]

    def kernel(me_ref, keep_ref, x_ref, y_ref, *out_refs):
        total = keep_ref[0].astype(f32) + x_ref[0].astype(f32) + y_ref[0].astype(f32)
        for r, out_ref in enumerate(out_refs):

            @pl.when(pl.program_id(0) == r)
            def _():
                out_ref[...] = total.astype(out_ref.dtype)

    spec = pl.BlockSpec((1, rows, n), lambda r, me_ref: ((me_ref[0] >> 1) ^ r, 0, 0))
    mine, *sends = pl.pallas_call(
        kernel,
        out_shape=[jax.ShapeDtypeStruct((rows, n), bf16 if r else f32) for r in range(half)],
        grid_spec=pltpu.PrefetchScalarGridSpec(
            num_scalar_prefetch=1,
            grid=(half,),
            in_specs=[spec] * 3,
            out_specs=[pl.BlockSpec((rows, n), lambda r, me_ref: (0, 0))] * half,
        ),
        cost_estimate=pl.CostEstimate(flops=0, transcendentals=0, bytes_accessed=8 * keep.size),
        name="sum_and_split",
    )(lax.axis_index("dp").astype(jnp.int32).reshape(1), keep, by_x, by_y)
    return mine, sends


def scatter_z(sends):
    return [swap_apart(send, 2 * (r + 1)) for r, send in enumerate(sends)]


def add_all(keep, got):
    for part in got:
        keep = keep + part.astype(f32)
    return keep


def attend(qkv, block=512, unroll=4):
    rows, cols = qkv.shape
    size = HEAD_DIM
    heads = cols // (3 * size)
    factor = size ** (-0.5) * log2_e

    def kernel(x_ref, mix_ref, lse_ref, q_s, k_s, v_s, o_s, l_s):
        i = pl.program_id(0)

        @pl.when(i == 0)
        def _():
            for h in range(heads):
                b = h * 3 * size
                q_s[h] = x_ref[:, b : b + size]
                k_s[h] = x_ref[:, b + size : b + 2 * size]
                v_s[h, :, :size] = x_ref[:, b + 2 * size : b + 3 * size]
                v_s[h, :, size:] = jnp.ones((rows, 8), bf16)

        def one(h):
            q = q_s[h, pl.ds(pl.multiple_of(i * block, block), block), :]
            scores = lax.dot_general(
                q, k_s[h], (((1,), (1,)), ((), ())), preferred_element_type=f32
            )
            top = jnp.max(scores, axis=-1, keepdims=True)
            probs = jnp.exp2((scores - top) * factor)
            out = jnp.dot(probs.astype(bf16), v_s[h], preferred_element_type=f32)
            total = out[:, size : size + 1]
            o_s[h] = (out[:, :size] / total).astype(bf16)
            l_s[h] = top * factor + jnp.log2(total)

        def body(g, _):
            for u in range(unroll):
                one(g * unroll + u)
            return 0

        lax.fori_loop(0, heads // unroll, body, 0)
        for h in range(heads):
            mix_ref[:, h * size : (h + 1) * size] = o_s[h]
            lse_ref[:, h : h + 1] = l_s[h]

    return pl.pallas_call(
        kernel,
        out_shape=(
            jax.ShapeDtypeStruct((rows, heads * size), bf16),
            jax.ShapeDtypeStruct((rows, heads), f32),
        ),
        grid=(rows // block,),
        in_specs=[pl.BlockSpec((rows, cols), lambda i: (0, 0))],
        out_specs=(
            pl.BlockSpec((block, heads * size), lambda i: (i, 0)),
            pl.BlockSpec((block, heads), lambda i: (i, 0)),
        ),
        scratch_shapes=[pltpu.VMEM((heads, rows, size), bf16)] * 2
        + [
            pltpu.VMEM((heads, rows, size + 8), bf16),
            pltpu.VMEM((heads, block, size), bf16),
            pltpu.VMEM((heads, block, 1), f32),
        ],
        compiler_params=pltpu.CompilerParams(vmem_limit_bytes=48 << 20),
        cost_estimate=pl.CostEstimate(
            flops=16 * heads * rows * rows * size,
            transcendentals=heads * rows * rows,
            bytes_accessed=rows * cols * 2 + rows * heads * size * 2,
        ),
        name="attend",
    )(qkv)


def attend_back(qkv, grad_mix, lse, first, heads, block=1024, unroll=2):
    rows, cols = qkv.shape
    size = HEAD_DIM
    all_heads = cols // (3 * size)
    factor = size ** (-0.5) * log2_e
    scale = size ** (-0.5)
    steps = rows // block

    def kernel(x_ref, g_ref, lse_ref, out_ref, q_s, k_s, v_s, g_s, dq_s, dk_s, dv_s):
        i = pl.program_id(0)

        @pl.when(i == 0)
        def _():
            for h in range(heads):
                b = (first + h) * 3 * size
                q_s[h] = x_ref[:, b : b + size]
                k_s[h] = x_ref[:, b + size : b + 2 * size]
                v_s[h] = x_ref[:, b + 2 * size : b + 3 * size]
                g_s[h] = g_ref[:, (first + h) * size : (first + h + 1) * size]
            dk_s[...] = jnp.zeros_like(dk_s)
            dv_s[...] = jnp.zeros_like(dv_s)

        at = pl.ds(pl.multiple_of(i * block, block), block)

        def one(h):
            q = q_s[h, at, :]
            g = g_s[h, at, :]
            k = k_s[h]
            scores = lax.dot_general(k, q, (((1,), (1,)), ((), ())), preferred_element_type=f32)
            probs = jnp.exp2(scores * factor - lse_ref[first + h, :, at])
            grad_probs = lax.dot_general(
                v_s[h], g, (((1,), (1,)), ((), ())), preferred_element_type=f32
            )
            inner = jnp.sum(probs * grad_probs, axis=0, keepdims=True)
            grad_scores = (probs * (grad_probs - inner)).astype(bf16)
            dv_s[h] += jnp.dot(probs.astype(bf16), g, preferred_element_type=f32)
            dk_s[h] += jnp.dot(grad_scores, q, preferred_element_type=f32)
            grad_q = lax.dot_general(
                grad_scores, k, (((0,), (0,)), ((), ())), preferred_element_type=f32
            )
            dq_s[h, at, :] = (grad_q * scale).astype(bf16)

        def body(g, _):
            for u in range(unroll):
                one(g * unroll + u)
            return 0

        lax.fori_loop(0, heads // unroll, body, 0)

        @pl.when(i == steps - 1)
        def _():
            for h in range(heads):
                b = h * 3 * size
                out_ref[:, b : b + size] = dq_s[h]
                out_ref[:, b + size : b + 2 * size] = (dk_s[h] * scale).astype(bf16)
                out_ref[:, b + 2 * size : b + 3 * size] = dv_s[h].astype(bf16)

    return pl.pallas_call(
        kernel,
        out_shape=jax.ShapeDtypeStruct((rows, heads * 3 * size), bf16),
        grid=(steps,),
        in_specs=[
            pl.BlockSpec((rows, cols), lambda i: (0, 0)),
            pl.BlockSpec((rows, all_heads * size), lambda i: (0, 0)),
            pl.BlockSpec((all_heads, 1, rows), lambda i: (0, 0, 0)),
        ],
        out_specs=pl.BlockSpec((rows, heads * 3 * size), lambda i: (0, 0)),
        scratch_shapes=[pltpu.VMEM((heads, rows, size), bf16)] * 5
        + [pltpu.VMEM((heads, rows, size), f32)] * 2,
        compiler_params=pltpu.CompilerParams(vmem_limit_bytes=56 << 20),
        cost_estimate=pl.CostEstimate(
            flops=40 * heads * rows * rows * size,
            transcendentals=heads * rows * rows,
            bytes_accessed=rows * cols * 4,
        ),
        name="attend_back",
    )(qkv, grad_mix, lse)


def shards(
    tokens_in,
    condition,
    w_ada,
    b_ada,
    w_qkv,
    b_qv,
    w_proj,
    b_proj,
    w_fc1,
    b_fc1,
    w_fc2,
    b_fc2,
    cotangent,
):
    tok_rows, width = tokens_in.shape
    head_size = HEAD_DIM
    dp_at = lax.axis_index("dp")
    t_at = lax.axis_index("tensor")
    y_at = t_at // 2
    core_at = t_at % 2
    dp_size = lax.axis_size("dp")
    ada_rows, ada_cols = w_ada.shape
    n_qkv, n_proj, n_fc1, n_fc2 = w_qkv.shape[1], w_proj.shape[0], w_fc1.shape[1], w_fc2.shape[0]
    n_bqv = b_qv.shape[0]
    heads = n_qkv // (3 * head_size)

    latents = condition.shape[0]
    cond_all = gather_small(condition)

    gather = lambda shard: lax.all_gather(shard, "dp", axis=0, tiled=True)
    qkv_all = gather(jnp.pad(w_qkv, ((0, 0), (0, -n_qkv % 128))))
    fc1_all = gather(w_fc1)
    fc2_mine, proj_mine = w_fc2.T, w_proj.T
    theirs = swap_y(jnp.concatenate([fc2_mine, proj_mine], axis=1))
    fc2_all = gather(jnp.concatenate([fc2_mine, theirs[:, :n_fc2]], axis=1))
    proj_z = gather_start(jnp.concatenate([proj_mine, theirs[:, n_fc2:]], axis=1))
    qkv_theirs = swap_y(qkv_all)
    qkv_near, qkv_far = ((qkv_all,), 0, n_qkv), ((qkv_theirs,), 0, n_qkv)
    fc2_near, fc2_far = ((fc2_all,), 0, n_fc2), ((fc2_all,), n_fc2, 2 * n_fc2)
    fc1_theirs = swap_y(after(fc1_all, qkv_theirs))
    fc1_near, fc1_far = ((fc1_all,), 0, n_fc1), ((fc1_theirs,), 0, n_fc1)

    inputs_theirs = swap_cores(jnp.concatenate([tokens_in, cotangent], axis=0))
    tokens_all = jnp.concatenate([tokens_in, inputs_theirs[:tok_rows]], axis=0)
    cot_all = jnp.concatenate([cotangent, inputs_theirs[tok_rows:]], axis=0)

    cond_vals = cond_all.astype(f32)
    silu_all = (cond_vals * jax.nn.sigmoid(cond_vals)).astype(bf16)
    silu_mine = lax.dynamic_slice_in_dim(silu_all, dp_at * ada_rows, ada_rows, 1)
    mod_part = jnp.dot(silu_mine, w_ada, preferred_element_type=f32)
    mod_part = mod_part + jnp.where(dp_at == 0, b_ada.astype(f32), 0.0)
    by_y = mod_part.reshape(dp_size, 2, ada_cols)
    mod_keep = lax.dynamic_index_in_dim(by_y, y_at, 1, True)
    mod_send = lax.dynamic_index_in_dim(by_y, 1 - y_at, 1, False)
    bias_mine = jnp.concatenate([b_qv, b_fc1]).astype(f32)[None]
    mod_got = swap_y(jnp.concatenate([mod_send, bias_mine], axis=0))
    bias_theirs = mod_got[dp_size:]
    mod_two = ordered(y_at, mod_keep, mod_got[:dp_size, None], 1)
    mod_all = ordered(core_at, mod_two[:, :, None], swap_cores(mod_two)[:, :, None], 2)
    mod_all = mod_all.reshape(dp_size, 4 * ada_cols)
    for bit in range(dp_bits()):
        pairs = mod_all.reshape(mod_all.shape[0] // 2, 2, 4 * ada_cols)
        keep = lax.dynamic_index_in_dim(pairs, own_bit(bit), 1, False)
        send = lax.dynamic_index_in_dim(pairs, 1 - own_bit(bit), 1, False)
        mod_all = keep + swap_dp(send, bit)
    mod_row = after(mod_all, tokens_all, cot_all)

    shift_attn, scale_attn, gate_attn, shift_mlp, scale_mlp, gate_mlp = jnp.split(mod_row, 6, axis=1)

    def qkv_bias(values):
        pair = values[0, :n_bqv].reshape(heads, 2, head_size)
        return jnp.stack([pair[:, 0], jnp.zeros_like(pair[:, 0]), pair[:, 1]], axis=1).reshape(1, n_qkv)

    attn_in, qkv_n = norm_project(tokens_all, scale_attn, shift_attn, qkv_bias(bias_mine), qkv_near)
    mix_n, lse_n = attend(qkv_n)
    proj_own = jnp.stack(after(proj_z, mix_n))
    proj_theirs = swap_dp(proj_own, 0)
    qkv_f = project(after(attn_in, mix_n, proj_own), qkv_bias(bias_theirs), qkv_far)
    mix_f, lse_f = attend(qkv_f)
    proj_all = gather_end(proj_own, after(proj_theirs, mix_f))
    proj_near, proj_far = ((proj_all,), 0, n_proj), ((proj_all,), n_proj, 2 * n_proj)
    proj_row = b_proj.astype(f32)[None]
    out_mine = project_out(mix_n, mix_f, proj_near, proj_far)
    out_theirs = swap_cores(out_mine)
    middle, mlp_in, grad_mlp, grad_b2 = middle_norm(
        out_mine, out_theirs, tokens_all, cot_all, proj_row,
        gate_attn, scale_mlp, shift_mlp, gate_mlp,
    )

    act_n, slope_n = feed_forward(mlp_in, bias_mine[:, n_bqv:], fc1_near)
    act_f, slope_f = feed_forward(after(mlp_in, act_n), bias_theirs[:, n_bqv:], fc1_far)

    fc2_term_f = weight_term(grad_mlp, act_f, bf16)
    fc2_far_keep, *sends = relay_first(fc2_term_f)
    by_x, by_y = swap_dp(sends[0], 0), swap_y(sends[1])
    fc2_term_n = weight_term(grad_mlp, act_n, f32)
    pre_n, grad_in_near, mlp_near, b1_n = feed_back(
        after(grad_mlp, fc2_term_n, fc2_far_keep, sends), act_n, slope_n, None, fc1_near, fc2_near, f32
    )
    by_x, by_y = after((by_x, by_y), grad_in_near)
    fc2_keep, *sends = relay_sends(fc2_term_n, fc2_far_keep, by_x, by_y)
    fc2_got = swap_dp(sends[0], 0), swap_y(sends[1])
    pre_f, grad_in_mine, mlp_part, b1_f = feed_back(
        after(grad_mlp, sends), act_f, slope_f, (grad_in_near, mlp_near), fc1_far, fc2_far, bf16
    )
    grad_in_theirs = swap_cores(grad_in_mine)
    fc1_term_f = weight_term(mlp_in, after(pre_f, grad_in_mine), bf16)
    fc1_far_keep, *sends = relay_first(fc1_term_f)
    by_x, by_y = swap_dp(sends[0], 0), swap_y(sends[1])
    fc1_term_n = weight_term(mlp_in, pre_n, f32)
    fc2_got = after(fc2_got, fc1_term_n)
    fc2_keep, z_sends = sum_and_split(fc2_keep, *fc2_got)
    grad_middle, grad_attn, gmix_n, gmix_f, mid_sums = middle_back(
        after(grad_in_mine, fc1_term_n, fc1_far_keep, sends, z_sends), grad_in_theirs, middle, cot_all,
        out_mine, out_theirs, proj_row, gate_attn, scale_mlp, proj_near, proj_far,
    )
    fc2_got = scatter_z(z_sends)

    proj_term_f = weight_term(grad_attn, mix_f, bf16)
    proj_term_n = weight_term(grad_attn, mix_n, f32)
    by_x, by_y = after((by_x, by_y), proj_term_n, fc2_got)
    fc1_keep, *sends = relay_sends(fc1_term_n, fc1_far_keep, by_x, by_y)
    fc1_got = swap_dp(sends[0], 0), swap_y(sends[1])
    rows_of = lambda lse: lse.T.reshape(heads, 1, 2 * tok_rows)
    grad_f = attend_back(
        qkv_f, after(gmix_f, proj_term_f, proj_term_n, sends), rows_of(lse_f), 0, heads
    )
    one_term_f = jnp.concatenate([weight_term(attn_in, grad_f, bf16), proj_term_f], axis=3)
    one_far_keep, *sends = relay_first(one_term_f)
    by_x, by_y = swap_dp(sends[0], 0), swap_y(sends[1])
    part_f = project_back(after(grad_f, sends), qkv_far, None, f32)
    fc1_got = after(fc1_got, part_f)
    fc1_keep, z_sends = sum_and_split(fc1_keep, *fc1_got)
    fc1_got = scatter_z(z_sends)
    grad_n = attend_back(
        qkv_n, after(gmix_n, part_f, one_far_keep, z_sends), rows_of(lse_n), 0, heads
    )
    attn_part = project_back(after(grad_n, by_x, by_y), qkv_near, part_f, bf16)
    attn_theirs = swap_cores(attn_part[tok_rows:])
    one_term_n = jnp.concatenate(
        [weight_term(after(attn_in, attn_part, fc1_got), grad_n, f32), proj_term_n], axis=3
    )
    one_keep, *sends = relay_sends(one_term_n, one_far_keep, by_x, by_y)
    one_got = swap_dp(sends[0], 0), swap_y(sends[1])
    grad_tokens, one_sums = first_back(
        after(attn_part, sends), attn_theirs, tokens_in, grad_middle, scale_attn
    )
    mlp_theirs = swap_cores(after(mlp_part[tok_rows:], grad_n))
    result, gate_sums = finish(mlp_part, mlp_theirs, middle, cotangent, b_fc2.astype(f32)[None], gate_mlp)

    def value_sums(grads):
        sums = jnp.sum(grads.astype(f32), axis=0).reshape(heads, 3, head_size)
        return jnp.concatenate([sums[:, :1], sums[:, 2:]], axis=1).reshape(n_bqv)

    mod_sums = jnp.concatenate([one_sums[:2].reshape(-1), mid_sums[2], mid_sums[0], mid_sums[1], gate_sums[0]])
    mod_sums = mod_sums + swap_cores(mod_sums)
    sums = jnp.concatenate(
        [value_sums(grad_n), b1_n[0], mid_sums[3], grad_b2[0], value_sums(grad_f), b1_f[0]]
    )
    grad_mod = mod_sums[None]
    for bit in list(range(1, dp_bits())) + [0]:
        size = grad_mod.size
        if bit == 2:
            grad_mod = after(grad_mod, one_got)
        if bit == 0:
            one_keep, one_sends = sum_and_split(one_keep, *one_got)
            grad_mod = after(grad_mod, one_sends)
        got = swap_dp(jnp.concatenate([grad_mod.reshape(size), sums]), bit)
        theirs = got[:size].reshape(grad_mod.shape)
        if bit == 0:
            both = jnp.where(own_bit(0) == 0, jnp.stack([grad_mod, theirs], 1), jnp.stack([theirs, grad_mod], 1))
            grad_mod = both.reshape(dp_size, 4, ada_cols)
        else:
            grad_mod = ordered(own_bit(bit), grad_mod, theirs, 0)
        sums = sums + got[size:]
    mod_keep = lax.dynamic_index_in_dim(grad_mod, t_at, 1, False)
    mod_send = lax.dynamic_index_in_dim(grad_mod, t_at ^ 2, 1, False)
    n_bias = n_bqv + n_fc1
    shared = n_bias + 2 * width
    got = swap_y(jnp.concatenate([mod_send.reshape(-1), sums[n_bias:shared], sums[shared:]]))
    mod_got, rest = got[: mod_send.size].reshape(mod_send.shape), got[mod_send.size :]
    bias_sums = sums[:n_bias] + rest[2 * width :]
    out_sums = sums[n_bias:shared] + rest[: 2 * width]
    grad_mod = ordered(y_at, mod_keep[:, None], mod_got[:, None], 1).reshape(2 * dp_size, ada_cols)
    one_got = scatter_z(one_sends)
    owned_ada = lax.dot_general(
        silu_mine.astype(f32), after(grad_mod, one_sends), (((0,), (0,)), ((), ())), precision=highest
    )
    grad_ba = jnp.sum(grad_mod, axis=0)
    silu_part = lax.dot_general(
        after(grad_mod, one_sends), w_ada.astype(f32), (((1,), (1,)), ((), ())), precision=highest
    )
    silu_part = silu_part + swap_cores(silu_part)
    silu_part = silu_part + swap_y(silu_part)
    owned_one = add_all(one_keep, one_got)
    grad_silu = exchange_small(silu_part.reshape(dp_size, latents, ada_rows))
    cond_vals = condition.astype(f32)
    cond_sigmoid = jax.nn.sigmoid(cond_vals)
    grad_condition = grad_silu * cond_sigmoid * (1.0 + cond_vals * (1.0 - cond_sigmoid))
    return (
        result,
        grad_tokens,
        grad_condition,
        owned_ada,
        grad_ba,
        owned_one[:, :n_qkv],
        bias_sums[:n_bqv],
        owned_one[:, n_qkv:].T,
        out_sums[:width],
        add_all(fc1_keep, fc1_got),
        bias_sums[n_bqv:],
        add_all(fc2_keep, fc2_got).T,
        out_sums[width:],
    )


def solution(mesh):
    placed = (
        P(("dp", "tensor"), None),
        P("dp", None),
        P("dp", "tensor"),
        P("tensor"),
        P("dp", "tensor"),
        P("tensor"),
        P("tensor", "dp"),
        P(),
        P("dp", "tensor"),
        P("tensor"),
        P("tensor", "dp"),
        P(),
        P(("dp", "tensor"), None),
    )
    return jax.shard_map(
        shards,
        mesh=mesh,
        in_specs=placed,
        out_specs=(
            P(("dp", "tensor"), None),
            P(("dp", "tensor"), None),
            P("dp", None),
            P("dp", "tensor"),
            P("tensor"),
            P("dp", "tensor"),
            P("tensor"),
            P("tensor", "dp"),
            P(),
            P("dp", "tensor"),
            P("tensor"),
            P("tensor", "dp"),
            P(),
        ),
        check_vma=False,
    )
```

```python
import jax
import jax.numpy as jnp
from jax import lax
from jax.experimental import pallas as pl
from jax.experimental.pallas import tpu as pltpu
from jax.sharding import PartitionSpec as P

HEAD_DIM = 72
SEQ = 1024

highest = lax.Precision.HIGHEST
root_two_pi = 0.7978845608028654
cubic_term = 0.044715
epsilon = 1e-06
log2_e = 1.4426950408889634
bf16 = jnp.bfloat16
f32 = jnp.float32


def swap_cores(values):
    return lax.ppermute(values, "tensor", [(i, i ^ 1) for i in range(4)])


def swap_y(values):
    return lax.ppermute(values, "tensor", [(i, i ^ 2) for i in range(4)])


def swap_apart(values, apart):
    size = lax.axis_size("dp")
    return lax.ppermute(values, "dp", [(i, i ^ apart) for i in range(size)])


def swap_dp(values, bit):
    return swap_apart(values, 1 << bit)


def swap_diagonal(values):
    size = 4 * lax.axis_size("dp")
    return lax.ppermute(values, ("dp", "tensor"), [(i, i ^ 6) for i in range(size)])


def after(values, *deps):
    return lax.optimization_barrier((values, deps))[0]


def dp_bits():
    return lax.axis_size("dp").bit_length() - 1


def own_bit(bit):
    return (lax.axis_index("dp") >> bit) & 1


def ordered(flag, mine, theirs, axis):
    first = jnp.where(flag == 0, mine, theirs)
    second = jnp.where(flag == 0, theirs, mine)
    return jnp.concatenate([first, second], axis=axis)


def gather_small(values):
    for bit in range(dp_bits()):
        values = ordered(own_bit(bit), values, swap_dp(values, bit), 0)
    return values


def scatter_small(values):
    for bit in reversed(range(dp_bits())):
        halves = values.reshape((2, values.shape[0] // 2) + values.shape[1:])
        mine = own_bit(bit)
        keep = lax.dynamic_index_in_dim(halves, mine, 0, False)
        send = lax.dynamic_index_in_dim(halves, 1 - mine, 0, False)
        values = keep + swap_dp(send, bit)
    return values


def exchange_small(values):
    dp, k, n = values.shape
    values = values[:, :, None]
    for bit in range(dp_bits()):
        pairs = values.reshape((values.shape[0] // 2, 2) + values.shape[1:])
        mine = own_bit(bit)
        keep = lax.dynamic_index_in_dim(pairs, mine, 1, False)
        send = lax.dynamic_index_in_dim(pairs, 1 - mine, 1, False)
        values = ordered(mine, keep, swap_dp(send, bit), 2)
    return values.reshape(k, dp * n)


def width_of(weight):
    return weight[2] - weight[1]


def height_of(weight):
    return sum(piece.shape[0] for piece in weight[0])


def row_step(
    body, rows, block, row_inputs, flat_inputs, weights, row_outputs, sum_outputs, name, flops=0
):
    steps = rows // block
    arrays, specs = [], []
    for entry in row_inputs:
        array, index = entry if isinstance(entry, tuple) else (entry, lambda i: i)
        arrays.append(array)
        specs.append(pl.BlockSpec((block, array.shape[1]), lambda i, index=index: (index(i), 0)))
    for array in flat_inputs:
        arrays.append(array)
        specs.append(pl.BlockSpec(array.shape, lambda i, nd=array.ndim: (0,) * nd))
    spans = [
        (lo // 128 * 128, min(-(-hi // 128) * 128, pieces[0].shape[1])) for pieces, lo, hi in weights
    ]
    counts = [len(pieces) for pieces, _, _ in weights]
    for pieces, _, _ in weights:
        arrays += pieces
        specs += [pl.BlockSpec(memory_space=pl.ANY)] * len(pieces)
    outs, out_specs = [], []
    for columns, kind in row_outputs:
        outs.append(jax.ShapeDtypeStruct((rows, columns), kind))
        out_specs.append(pl.BlockSpec((block, columns), lambda i: (i, 0)))
    for count, columns in sum_outputs:
        outs.append(jax.ShapeDtypeStruct((count, columns), f32))
        out_specs.append(pl.BlockSpec((count, columns), lambda i: (0, 0)))
    scratch = []
    for weight, (lo, hi) in zip(weights, spans):
        scratch += [pltpu.VMEM((height_of(weight), hi - lo), bf16), pltpu.SemaphoreType.DMA((len(weight[0]),))]
    n_row, n_flat = len(row_inputs), len(flat_inputs)

    def kernel(*refs):
        refs = list(refs)

        def take(count):
            part = refs[:count]
            del refs[:count]
            return part

        row_refs, flat_refs = take(n_row), take(n_flat)
        weight_refs = [take(count) for count in counts]
        out_refs, sum_refs = take(len(row_outputs)), take(len(sum_outputs))
        targets = [take(2) for _ in weights]
        step = pl.program_id(0)

        @pl.when(step == 0)
        def _():
            copies = []
            for refs, (target, sems), (lo, hi) in zip(weight_refs, targets, spans):
                at = 0
                for i, ref in enumerate(refs):
                    rows = ref.shape[0]
                    copies.append(
                        pltpu.make_async_copy(
                            ref.at[:, lo:hi], target.at[at : at + rows], sems.at[i]
                        )
                    )
                    at += rows
            for copy in copies:
                copy.start()
            for ref in sum_refs:
                ref[...] = jnp.zeros_like(ref)
            for copy in copies:
                copy.wait()

        views = [
            target.at[:, lo - at : hi - at]
            for (target, _), (_, lo, hi), (at, _) in zip(targets, weights, spans)
        ]
        body(step, row_refs, flat_refs, views, out_refs, sum_refs)

    moved = sum(a.size * a.dtype.itemsize for a in arrays) + sum(
        o.size * o.dtype.itemsize for o in outs
    )
    return pl.pallas_call(
        kernel,
        out_shape=outs,
        grid=(steps,),
        in_specs=specs,
        out_specs=out_specs,
        scratch_shapes=scratch,
        compiler_params=pltpu.CompilerParams(vmem_limit_bytes=58 << 20),
        cost_estimate=pl.CostEstimate(flops=flops, transcendentals=0, bytes_accessed=moved),
        name=name,
    )(*arrays)


def dot_nt(left_rows, right_mat):
    return lax.dot_general(
        left_rows, right_mat, (((1,), (1,)), ((), ())), preferred_element_type=f32
    )


def dot_nn(left_rows, right_mat):
    return jnp.dot(left_rows, right_mat, preferred_element_type=f32)


def normed_of(values):
    centre = values - jnp.mean(values, axis=-1, keepdims=True)
    inverse = lax.rsqrt(jnp.mean(centre * centre, axis=-1, keepdims=True) + epsilon)
    return centre * inverse, inverse


def norm_back(normed, inverse, grad_in):
    mean_grad = jnp.mean(grad_in, axis=-1, keepdims=True)
    mean_cross = jnp.mean(grad_in * normed, axis=-1, keepdims=True)
    return inverse * (grad_in - mean_grad - normed * mean_cross)


def rows_sum(values):
    return jnp.sum(values, axis=0, keepdims=True)


def norm_project(tokens, scale, shift, bias, weight):
    rows, width = tokens.shape
    n = width_of(weight)

    def body(step, ins, flat, w, outs, sums):
        normed, _ = normed_of(ins[0][...].astype(f32))
        attn_in = (normed * (1.0 + flat[0][...]) + flat[1][...]).astype(bf16)
        outs[0][...] = attn_in
        outs[1][...] = (dot_nn(attn_in, w[0][...]) + flat[2][...]).astype(bf16)

    return row_step(
        body, rows, 256, [tokens], [scale, shift, bias], [weight],
        [(width, bf16), (n, bf16)], [], "norm_project",
    )


def project(values, bias, weight):
    n = width_of(weight)

    def body(step, ins, flat, w, outs, sums):
        outs[0][...] = (dot_nn(ins[0][...], w[0][...]) + flat[0][...]).astype(bf16)

    return row_step(body, values.shape[0], 256, [values], [bias], [weight], [(n, bf16)], [], "project")[0]


def project_out(mix_near, mix_far, near, far):
    def body(step, ins, flat, w, outs, sums):
        total = dot_nt(ins[0][...], w[0][...]) + dot_nt(ins[1][...], w[1][...])
        outs[0][...] = total.astype(bf16)

    width = height_of(near)
    rows = mix_near.shape[0]
    return row_step(
        body, rows, 256, [mix_near, mix_far], [], [near, far], [(width, bf16)], [], "project_out"
    )[0]


def other_half(steps):
    return lambda i: jnp.where(i < steps // 2, i + steps // 2, i - steps // 2)


def middle_norm(mine, theirs, tokens, cotangent, b_proj, gate_attn, scale_mlp, shift_mlp, gate_mlp):
    rows, width = tokens.shape
    block = 256

    def body(step, ins, flat, w, outs, sums):
        attn_out = ins[0][...].astype(f32) + ins[1][...].astype(f32) + flat[0][...]
        middle = ins[2][...].astype(f32) + flat[1][...] * attn_out
        outs[0][...] = middle
        normed, _ = normed_of(middle)
        outs[1][...] = (normed * (1.0 + flat[2][...]) + flat[3][...]).astype(bf16)
        grad_mlp = (flat[4][...] * ins[3][...].astype(f32)).astype(bf16)
        outs[2][...] = grad_mlp
        sums[0][...] += rows_sum(grad_mlp.astype(f32))

    return row_step(
        body, rows, block, [mine, (theirs, other_half(rows // block)), tokens, cotangent],
        [b_proj, gate_attn, scale_mlp, shift_mlp, gate_mlp], [],
        [(width, f32), (width, bf16), (width, bf16)], [(1, width)], "middle_norm",
    )


def gelu_parts(pre_act):
    tangent = jnp.tanh(root_two_pi * (pre_act + cubic_term * pre_act * pre_act * pre_act))
    activated = 0.5 * pre_act * (1.0 + tangent)
    gelu_slope = 0.5 * (1.0 + tangent) + 0.5 * pre_act * (1.0 - tangent * tangent) * root_two_pi * (
        1.0 + 3.0 * cubic_term * pre_act * pre_act
    )
    return activated, gelu_slope


def feed_forward(mlp_in, bias, weight):
    n = width_of(weight)

    def body(step, ins, flat, w, outs, sums):
        activated, slope = gelu_parts(dot_nn(ins[0][...], w[0][...]) + flat[0][...])
        outs[0][...] = activated.astype(bf16)
        outs[1][...] = slope

    return row_step(
        body, mlp_in.shape[0], 256, [mlp_in], [bias], [weight], [(n, bf16), (n, f32)], [], "feed_forward"
    )


def feed_back(grad_mlp, act, slope, added, fc1, fc2, kind):
    rows, width = grad_mlp.shape
    n = act.shape[1]

    def body(step, ins, flat, w, outs, sums):
        grad_pre = (dot_nn(ins[0][...], w[1][...]) * ins[2][...]).astype(bf16)
        outs[0][...] = grad_pre
        sums[0][...] += rows_sum(grad_pre.astype(f32))
        grad_in = dot_nt(grad_pre, w[0][...])
        out = dot_nt(ins[1][...], w[1][...])
        if added is not None:
            grad_in = grad_in + ins[3][...]
            out = out + ins[4][...]
        outs[1][...] = grad_in.astype(kind)
        outs[2][...] = out.astype(kind)

    return row_step(
        body, rows, 256, [grad_mlp, act, slope] + ([] if added is None else list(added)), [], [fc1, fc2],
        [(n, bf16), (width, kind), (width, kind)], [(1, n)], "feed_back",
    )


def middle_back(
    grad_mine, grad_theirs, middle, cotangent, mine, theirs, b_proj, gate_attn, scale_mlp, near, far
):
    rows, width = middle.shape
    block = 256
    steps = rows // block
    n = width_of(near)

    def body(step, ins, flat, w, outs, sums):
        grad_in = ins[0][...].astype(f32) + ins[1][...].astype(f32)
        normed, inverse = normed_of(ins[2][...])
        grad_middle = ins[3][...].astype(f32) + norm_back(
            normed, inverse, grad_in * (1.0 + flat[2][...])
        )
        outs[0][...] = grad_middle
        grad_attn = (flat[1][...] * grad_middle).astype(bf16)
        outs[1][...] = grad_attn
        outs[2][...] = dot_nn(grad_attn, w[0][...]).astype(bf16)
        outs[3][...] = dot_nn(grad_attn, w[1][...]).astype(bf16)
        sums[0][3:4] += rows_sum(grad_attn.astype(f32))

        @pl.when(step < steps // 2)
        def _():
            attn_out = ins[4][...].astype(f32) + ins[5][...].astype(f32) + flat[0][...]
            sums[0][0:1] += rows_sum(grad_in)
            sums[0][1:2] += rows_sum(grad_in * normed)
            sums[0][2:3] += rows_sum(grad_middle * attn_out)

    flip = other_half(steps)
    return row_step(
        body, rows, block,
        [grad_mine, (grad_theirs, flip), middle, cotangent, mine, (theirs, flip)],
        [b_proj, gate_attn, scale_mlp], [near, far],
        [(width, f32), (width, bf16), (n, bf16), (n, bf16)], [(8, width)], "middle_back",
    )


def project_back(grads, weight, added, kind):
    width = height_of(weight)

    def body(step, ins, flat, w, outs, sums):
        total = dot_nt(ins[0][...], w[0][...])
        if added is not None:
            total = total + ins[1][...]
        outs[0][...] = total.astype(kind)

    inputs = [grads] if added is None else [grads, added]
    return row_step(
        body, grads.shape[0], 256, inputs, [], [weight], [(width, kind)], [], "project_back"
    )[0]


def first_back(mine, theirs, tokens, grad_middle, scale_attn):
    rows, width = tokens.shape

    def body(step, ins, flat, w, outs, sums):
        grad_in = ins[0][...].astype(f32) + ins[1][...].astype(f32)
        normed, inverse = normed_of(ins[2][...].astype(f32))
        outs[0][...] = ins[3][...] + norm_back(normed, inverse, grad_in * (1.0 + flat[0][...]))
        sums[0][0:1] += rows_sum(grad_in)
        sums[0][1:2] += rows_sum(grad_in * normed)

    return row_step(
        body, rows, 256, [mine, theirs, tokens, grad_middle], [scale_attn], [],
        [(width, f32)], [(8, width)], "first_back",
    )


def finish(mine, theirs, middle, cotangent, b_fc2, gate_mlp):
    rows, width = cotangent.shape

    def body(step, ins, flat, w, outs, sums):
        mlp_out = ins[0][...].astype(f32) + ins[1][...].astype(f32) + flat[0][...]
        outs[0][...] = (ins[2][...] + flat[1][...] * mlp_out).astype(bf16)
        sums[0][...] += rows_sum(ins[3][...].astype(f32) * mlp_out)

    return row_step(
        body, rows, 256, [mine, theirs, middle, cotangent], [b_fc2, gate_mlp], [],
        [(width, bf16)], [(1, width)], "finish",
    )


def gather_start(shard):
    half = lax.axis_size("dp") // 2
    if half <= 4:
        return [shard] + [swap_apart(shard, 2 * r) for r in range(1, half)]
    blocks = shard[None]
    for bit in range(1, dp_bits()):
        blocks = jnp.concatenate([blocks, swap_dp(blocks, bit)], axis=0)
    return list(blocks)


def gather_end(mine, theirs):
    half, rows, n = mine.shape
    blocks = jnp.stack([mine, theirs], axis=1).reshape(2 * half, rows, n)
    for bit in range(dp_bits()):
        pairs = blocks.reshape(half >> bit, 2, 1 << bit, rows, n)
        blocks = jnp.where(own_bit(bit) == 0, pairs, pairs[:, ::-1]).reshape(blocks.shape)
    return blocks.reshape(2 * half * rows, n)


def split_bit(blocks, axis, bit):
    mine = own_bit(bit)
    keep = lax.dynamic_index_in_dim(blocks, mine, axis, False)
    send = lax.dynamic_index_in_dim(blocks, 1 - mine, axis, False)
    return keep, send.astype(bf16)


def weight_term(left, right, kind):
    out = lax.dot_general(left, right, (((0,), (0,)), ((), ())), preferred_element_type=f32)
    dp = lax.axis_size("dp")
    return out.astype(kind).reshape(dp // 2, 2, out.shape[0] // dp, out.shape[1])


def relay_first(far):
    keep, other = split_bit(far, 1, 0)
    half = other.shape[0] // 2
    return keep, other[:half], other[half:]


def relay_sends(near, far_keep, by_x, by_y):
    near_keep, near_other = split_bit(near, 1, 0)
    half = by_x.shape[0]
    to_x = jnp.concatenate([near_other[:half], near_other[half:] + by_y], axis=0)
    to_y = jnp.concatenate([far_keep[:half] + by_x, far_keep[half:]], axis=0)
    return near_keep, to_x, to_y


def scatter_z_sends(total):
    half = total.shape[0]
    if half > 4:
        for bit in range(dp_bits() - 1, 1, -1):
            blocks = total.reshape((2, total.shape[0] // 2) + total.shape[1:])
            keep, send = split_bit(blocks, 0, bit)
            total = keep + swap_dp(send, bit).astype(f32)
        keep, send = split_bit(total, 0, 1)
        return keep, [send]
    here = lax.axis_index("dp") >> 1
    sends = [
        lax.dynamic_index_in_dim(total, here ^ r, 0, False).astype(bf16) for r in range(1, half)
    ]
    return lax.dynamic_index_in_dim(total, here, 0, False), sends


def sum_and_split(keep, by_x, by_y):
    half, rows, n = keep.shape
    if half > 4:
        total = add_all(keep.astype(f32), (by_x, by_y))
        for bit in range(dp_bits() - 1, 1, -1):
            blocks = total.reshape((2, total.shape[0] // 2) + total.shape[1:])
            keep, send = split_bit(blocks, 0, bit)
            total = keep + swap_dp(send, bit).astype(f32)
        keep, send = split_bit(total, 0, 1)
        return keep, [send]

    def kernel(me_ref, keep_ref, x_ref, y_ref, *out_refs):
        total = keep_ref[0].astype(f32) + x_ref[0].astype(f32) + y_ref[0].astype(f32)
        for r, out_ref in enumerate(out_refs):

            @pl.when(pl.program_id(0) == r)
            def _():
                out_ref[...] = total.astype(out_ref.dtype)

    spec = pl.BlockSpec((1, rows, n), lambda r, me_ref: ((me_ref[0] >> 1) ^ r, 0, 0))
    mine, *sends = pl.pallas_call(
        kernel,
        out_shape=[jax.ShapeDtypeStruct((rows, n), bf16 if r else f32) for r in range(half)],
        grid_spec=pltpu.PrefetchScalarGridSpec(
            num_scalar_prefetch=1,
            grid=(half,),
            in_specs=[spec] * 3,
            out_specs=[pl.BlockSpec((rows, n), lambda r, me_ref: (0, 0))] * half,
        ),
        cost_estimate=pl.CostEstimate(flops=0, transcendentals=0, bytes_accessed=8 * keep.size),
        name="sum_and_split",
    )(lax.axis_index("dp").astype(jnp.int32).reshape(1), keep, by_x, by_y)
    return mine, sends


def scatter_z(sends):
    return [swap_apart(send, 2 * (r + 1)) for r, send in enumerate(sends)]


def add_all(keep, got):
    for part in got:
        keep = keep + part.astype(f32)
    return keep


def attend(qkv, block=512, unroll=4):
    rows, cols = qkv.shape
    size = HEAD_DIM
    heads = cols // (3 * size)
    factor = size ** (-0.5) * log2_e

    def kernel(x_ref, mix_ref, lse_ref, q_s, k_s, v_s, o_s, l_s):
        i = pl.program_id(0)

        @pl.when(i == 0)
        def _():
            for h in range(heads):
                b = h * 3 * size
                q_s[h] = x_ref[:, b : b + size]
                k_s[h] = x_ref[:, b + size : b + 2 * size]
                v_s[h, :, :size] = x_ref[:, b + 2 * size : b + 3 * size]
                v_s[h, :, size:] = jnp.ones((rows, 8), bf16)

        def one(h):
            q = q_s[h, pl.ds(pl.multiple_of(i * block, block), block), :]
            scores = lax.dot_general(
                q, k_s[h], (((1,), (1,)), ((), ())), preferred_element_type=f32
            )
            top = jnp.max(scores, axis=-1, keepdims=True)
            probs = jnp.exp2((scores - top) * factor)
            out = jnp.dot(probs.astype(bf16), v_s[h], preferred_element_type=f32)
            total = out[:, size : size + 1]
            o_s[h] = (out[:, :size] / total).astype(bf16)
            l_s[h] = top * factor + jnp.log2(total)

        def body(g, _):
            for u in range(unroll):
                one(g * unroll + u)
            return 0

        lax.fori_loop(0, heads // unroll, body, 0)
        for h in range(heads):
            mix_ref[:, h * size : (h + 1) * size] = o_s[h]
            lse_ref[:, h : h + 1] = l_s[h]

    return pl.pallas_call(
        kernel,
        out_shape=(
            jax.ShapeDtypeStruct((rows, heads * size), bf16),
            jax.ShapeDtypeStruct((rows, heads), f32),
        ),
        grid=(rows // block,),
        in_specs=[pl.BlockSpec((rows, cols), lambda i: (0, 0))],
        out_specs=(
            pl.BlockSpec((block, heads * size), lambda i: (i, 0)),
            pl.BlockSpec((block, heads), lambda i: (i, 0)),
        ),
        scratch_shapes=[pltpu.VMEM((heads, rows, size), bf16)] * 2
        + [
            pltpu.VMEM((heads, rows, size + 8), bf16),
            pltpu.VMEM((heads, block, size), bf16),
            pltpu.VMEM((heads, block, 1), f32),
        ],
        compiler_params=pltpu.CompilerParams(vmem_limit_bytes=48 << 20),
        cost_estimate=pl.CostEstimate(
            flops=16 * heads * rows * rows * size,
            transcendentals=heads * rows * rows,
            bytes_accessed=rows * cols * 2 + rows * heads * size * 2,
        ),
        name="attend",
    )(qkv)


def attend_back(qkv, grad_mix, lse, first, heads, block=1024, unroll=4):
    rows, cols = qkv.shape
    size = HEAD_DIM
    all_heads = cols // (3 * size)
    factor = size ** (-0.5) * log2_e
    scale = size ** (-0.5)
    steps = rows // block

    def kernel(x_ref, g_ref, lse_ref, out_ref, q_s, k_s, v_s, g_s, dq_s, dk_s, dv_s):
        i = pl.program_id(0)

        @pl.when(i == 0)
        def _():
            for h in range(heads):
                b = (first + h) * 3 * size
                q_s[h] = x_ref[:, b : b + size]
                k_s[h] = x_ref[:, b + size : b + 2 * size]
                v_s[h] = x_ref[:, b + 2 * size : b + 3 * size]
                g_s[h] = g_ref[:, (first + h) * size : (first + h + 1) * size]
            dk_s[...] = jnp.zeros_like(dk_s)
            dv_s[...] = jnp.zeros_like(dv_s)

        at = pl.ds(pl.multiple_of(i * block, block), block)

        def one(h):
            q = q_s[h, at, :]
            g = g_s[h, at, :]
            k = k_s[h]
            scores = lax.dot_general(k, q, (((1,), (1,)), ((), ())), preferred_element_type=f32)
            probs = jnp.exp2(scores * factor - lse_ref[first + h, :, at])
            grad_probs = lax.dot_general(
                v_s[h], g, (((1,), (1,)), ((), ())), preferred_element_type=f32
            )
            inner = jnp.sum(probs * grad_probs, axis=0, keepdims=True)
            grad_scores = (probs * (grad_probs - inner)).astype(bf16)
            dv_s[h] += jnp.dot(probs.astype(bf16), g, preferred_element_type=f32)
            dk_s[h] += jnp.dot(grad_scores, q, preferred_element_type=f32)
            grad_q = lax.dot_general(
                grad_scores, k, (((0,), (0,)), ((), ())), preferred_element_type=f32
            )
            dq_s[h, at, :] = (grad_q * scale).astype(bf16)

        def body(g, _):
            for u in range(unroll):
                one(g * unroll + u)
            return 0

        lax.fori_loop(0, heads // unroll, body, 0)

        @pl.when(i == steps - 1)
        def _():
            for h in range(heads):
                b = h * 3 * size
                out_ref[:, b : b + size] = dq_s[h]
                out_ref[:, b + size : b + 2 * size] = (dk_s[h] * scale).astype(bf16)
                out_ref[:, b + 2 * size : b + 3 * size] = dv_s[h].astype(bf16)

    return pl.pallas_call(
        kernel,
        out_shape=jax.ShapeDtypeStruct((rows, heads * 3 * size), bf16),
        grid=(steps,),
        in_specs=[
            pl.BlockSpec((rows, cols), lambda i: (0, 0)),
            pl.BlockSpec((rows, all_heads * size), lambda i: (0, 0)),
            pl.BlockSpec((all_heads, 1, rows), lambda i: (0, 0, 0)),
        ],
        out_specs=pl.BlockSpec((rows, heads * 3 * size), lambda i: (0, 0)),
        scratch_shapes=[pltpu.VMEM((heads, rows, size), bf16)] * 5
        + [pltpu.VMEM((heads, rows, size), f32)] * 2,
        compiler_params=pltpu.CompilerParams(vmem_limit_bytes=56 << 20),
        cost_estimate=pl.CostEstimate(
            flops=40 * heads * rows * rows * size,
            transcendentals=heads * rows * rows,
            bytes_accessed=rows * cols * 4,
        ),
        name="attend_back",
    )(qkv, grad_mix, lse)


def shards(
    tokens_in,
    condition,
    w_ada,
    b_ada,
    w_qkv,
    b_qv,
    w_proj,
    b_proj,
    w_fc1,
    b_fc1,
    w_fc2,
    b_fc2,
    cotangent,
):
    tok_rows, width = tokens_in.shape
    head_size = HEAD_DIM
    dp_at = lax.axis_index("dp")
    t_at = lax.axis_index("tensor")
    y_at = t_at // 2
    core_at = t_at % 2
    dp_size = lax.axis_size("dp")
    ada_rows, ada_cols = w_ada.shape
    n_qkv, n_proj, n_fc1, n_fc2 = w_qkv.shape[1], w_proj.shape[0], w_fc1.shape[1], w_fc2.shape[0]
    n_bqv = b_qv.shape[0]
    heads = n_qkv // (3 * head_size)

    latents = condition.shape[0]
    cond_all = gather_small(condition)

    gather = lambda shard: lax.all_gather(shard, "dp", axis=0, tiled=True)
    qkv_all = gather(jnp.pad(w_qkv, ((0, 0), (0, -n_qkv % 128))))
    fc1_all = gather(w_fc1)
    fc2_mine, proj_mine = w_fc2.T, w_proj.T
    theirs = swap_y(jnp.concatenate([fc2_mine, proj_mine], axis=1))
    fc2_all = gather(jnp.concatenate([fc2_mine, theirs[:, :n_fc2]], axis=1))
    proj_z = gather_start(jnp.concatenate([proj_mine, theirs[:, n_fc2:]], axis=1))
    qkv_theirs = swap_y(qkv_all)
    qkv_near, qkv_far = ((qkv_all,), 0, n_qkv), ((qkv_theirs,), 0, n_qkv)
    fc2_near, fc2_far = ((fc2_all,), 0, n_fc2), ((fc2_all,), n_fc2, 2 * n_fc2)
    fc1_theirs = swap_y(after(fc1_all, qkv_theirs))
    fc1_near, fc1_far = ((fc1_all,), 0, n_fc1), ((fc1_theirs,), 0, n_fc1)

    inputs_theirs = swap_cores(jnp.concatenate([tokens_in, cotangent], axis=0))
    tokens_all = jnp.concatenate([tokens_in, inputs_theirs[:tok_rows]], axis=0)
    cot_all = jnp.concatenate([cotangent, inputs_theirs[tok_rows:]], axis=0)

    cond_vals = cond_all.astype(f32)
    silu_all = (cond_vals * jax.nn.sigmoid(cond_vals)).astype(bf16)
    silu_mine = lax.dynamic_slice_in_dim(silu_all, dp_at * ada_rows, ada_rows, 1)
    mod_part = jnp.dot(silu_mine, w_ada, preferred_element_type=f32)
    mod_part = mod_part + jnp.where(dp_at == 0, b_ada.astype(f32), 0.0)
    by_y = mod_part.reshape(dp_size, 2, ada_cols)
    mod_keep = lax.dynamic_index_in_dim(by_y, y_at, 1, True)
    mod_send = lax.dynamic_index_in_dim(by_y, 1 - y_at, 1, False)
    bias_mine = jnp.concatenate([b_qv, b_fc1]).astype(f32)[None]
    mod_got = swap_y(jnp.concatenate([mod_send, bias_mine], axis=0))
    bias_theirs = mod_got[dp_size:]
    mod_two = ordered(y_at, mod_keep, mod_got[:dp_size, None], 1)
    mod_all = ordered(core_at, mod_two[:, :, None], swap_cores(mod_two)[:, :, None], 2)
    mod_all = mod_all.reshape(dp_size, 4 * ada_cols)
    for bit in range(dp_bits()):
        pairs = mod_all.reshape(mod_all.shape[0] // 2, 2, 4 * ada_cols)
        keep = lax.dynamic_index_in_dim(pairs, own_bit(bit), 1, False)
        send = lax.dynamic_index_in_dim(pairs, 1 - own_bit(bit), 1, False)
        mod_all = keep + swap_dp(send, bit)
    mod_row = after(mod_all, tokens_all, cot_all)

    shift_attn, scale_attn, gate_attn, shift_mlp, scale_mlp, gate_mlp = jnp.split(mod_row, 6, axis=1)

    def qkv_bias(values):
        pair = values[0, :n_bqv].reshape(heads, 2, head_size)
        return jnp.stack([pair[:, 0], jnp.zeros_like(pair[:, 0]), pair[:, 1]], axis=1).reshape(1, n_qkv)

    attn_in, qkv_n = norm_project(tokens_all, scale_attn, shift_attn, qkv_bias(bias_mine), qkv_near)
    mix_n, lse_n = attend(qkv_n)
    proj_own = jnp.stack(after(proj_z, mix_n))
    proj_theirs = swap_dp(proj_own, 0)
    qkv_f = project(after(attn_in, mix_n, proj_own), qkv_bias(bias_theirs), qkv_far)
    mix_f, lse_f = attend(qkv_f)
    proj_all = gather_end(proj_own, after(proj_theirs, mix_f))
    proj_near, proj_far = ((proj_all,), 0, n_proj), ((proj_all,), n_proj, 2 * n_proj)
    proj_row = b_proj.astype(f32)[None]
    out_mine = project_out(mix_n, mix_f, proj_near, proj_far)
    out_theirs = swap_cores(out_mine)
    middle, mlp_in, grad_mlp, grad_b2 = middle_norm(
        out_mine, out_theirs, tokens_all, cot_all, proj_row,
        gate_attn, scale_mlp, shift_mlp, gate_mlp,
    )

    act_n, slope_n = feed_forward(mlp_in, bias_mine[:, n_bqv:], fc1_near)
    act_f, slope_f = feed_forward(after(mlp_in, act_n), bias_theirs[:, n_bqv:], fc1_far)

    fc2_term_f = weight_term(grad_mlp, act_f, bf16)
    fc2_far_keep, *sends = relay_first(fc2_term_f)
    by_x, by_y = swap_dp(sends[0], 0), swap_y(sends[1])
    fc2_term_n = weight_term(grad_mlp, act_n, f32)
    pre_n, grad_in_near, mlp_near, b1_n = feed_back(
        after(grad_mlp, fc2_term_n, fc2_far_keep, sends), act_n, slope_n, None, fc1_near, fc2_near, f32
    )
    by_x, by_y = after((by_x, by_y), grad_in_near)
    fc2_keep, *sends = relay_sends(fc2_term_n, fc2_far_keep, by_x, by_y)
    fc2_got = swap_dp(sends[0], 0), swap_y(sends[1])
    pre_f, grad_in_mine, mlp_part, b1_f = feed_back(
        after(grad_mlp, sends), act_f, slope_f, (grad_in_near, mlp_near), fc1_far, fc2_far, bf16
    )
    grad_in_theirs = swap_cores(grad_in_mine)
    fc1_term_f = weight_term(mlp_in, after(pre_f, grad_in_mine), bf16)
    fc1_far_keep, *sends = relay_first(fc1_term_f)
    by_x, by_y = swap_dp(sends[0], 0), swap_y(sends[1])
    fc1_term_n = weight_term(mlp_in, pre_n, f32)
    fc2_got = after(fc2_got, fc1_term_n)
    fc2_keep, z_sends = sum_and_split(fc2_keep, *fc2_got)
    grad_middle, grad_attn, gmix_n, gmix_f, mid_sums = middle_back(
        after(grad_in_mine, fc1_term_n, fc1_far_keep, sends, z_sends), grad_in_theirs, middle, cot_all,
        out_mine, out_theirs, proj_row, gate_attn, scale_mlp, proj_near, proj_far,
    )
    fc2_got = scatter_z(z_sends)

    proj_term_f = weight_term(grad_attn, mix_f, bf16)
    proj_term_n = weight_term(grad_attn, mix_n, f32)
    by_x, by_y = after((by_x, by_y), proj_term_n, fc2_got)
    fc1_keep, *sends = relay_sends(fc1_term_n, fc1_far_keep, by_x, by_y)
    fc1_got = swap_dp(sends[0], 0), swap_y(sends[1])
    rows_of = lambda lse: lse.T.reshape(heads, 1, 2 * tok_rows)
    grad_f = attend_back(
        qkv_f, after(gmix_f, proj_term_f, proj_term_n, sends), rows_of(lse_f), 0, heads
    )
    one_term_f = jnp.concatenate([weight_term(attn_in, grad_f, bf16), proj_term_f], axis=3)
    one_far_keep, *sends = relay_first(one_term_f)
    by_x, by_y = swap_dp(sends[0], 0), swap_y(sends[1])
    part_f = project_back(after(grad_f, sends), qkv_far, None, f32)
    fc1_got = after(fc1_got, part_f)
    fc1_keep, z_sends = sum_and_split(fc1_keep, *fc1_got)
    fc1_got = scatter_z(z_sends)
    grad_n = attend_back(
        qkv_n, after(gmix_n, part_f, one_far_keep, z_sends), rows_of(lse_n), 0, heads
    )
    attn_part = project_back(after(grad_n, by_x, by_y), qkv_near, part_f, bf16)
    attn_theirs = swap_cores(attn_part[tok_rows:])
    one_term_n = jnp.concatenate(
        [weight_term(after(attn_in, attn_part, fc1_got), grad_n, f32), proj_term_n], axis=3
    )
    one_keep, *sends = relay_sends(one_term_n, one_far_keep, by_x, by_y)
    one_got = swap_dp(sends[0], 0), swap_y(sends[1])
    grad_tokens, one_sums = first_back(
        after(attn_part, sends), attn_theirs, tokens_in, grad_middle, scale_attn
    )
    mlp_theirs = swap_cores(after(mlp_part[tok_rows:], grad_n))
    result, gate_sums = finish(mlp_part, mlp_theirs, middle, cotangent, b_fc2.astype(f32)[None], gate_mlp)

    def value_sums(grads):
        sums = jnp.sum(grads.astype(f32), axis=0).reshape(heads, 3, head_size)
        return jnp.concatenate([sums[:, :1], sums[:, 2:]], axis=1).reshape(n_bqv)

    mod_sums = jnp.concatenate([one_sums[:2].reshape(-1), mid_sums[2], mid_sums[0], mid_sums[1], gate_sums[0]])
    mod_sums = mod_sums + swap_cores(mod_sums)
    sums = jnp.concatenate(
        [value_sums(grad_n), b1_n[0], mid_sums[3], grad_b2[0], value_sums(grad_f), b1_f[0]]
    )
    grad_mod = mod_sums[None]
    for bit in list(range(1, dp_bits())) + [0]:
        size = grad_mod.size
        if bit == 2:
            grad_mod = after(grad_mod, one_got)
        if bit == 0:
            one_keep, one_sends = sum_and_split(one_keep, *one_got)
            grad_mod = after(grad_mod, one_sends)
        got = swap_dp(jnp.concatenate([grad_mod.reshape(size), sums]), bit)
        theirs = got[:size].reshape(grad_mod.shape)
        if bit == 0:
            both = jnp.where(own_bit(0) == 0, jnp.stack([grad_mod, theirs], 1), jnp.stack([theirs, grad_mod], 1))
            grad_mod = both.reshape(dp_size, 4, ada_cols)
        else:
            grad_mod = ordered(own_bit(bit), grad_mod, theirs, 0)
        sums = sums + got[size:]
    mod_keep = lax.dynamic_index_in_dim(grad_mod, t_at, 1, False)
    mod_send = lax.dynamic_index_in_dim(grad_mod, t_at ^ 2, 1, False)
    n_bias = n_bqv + n_fc1
    shared = n_bias + 2 * width
    got = swap_y(jnp.concatenate([mod_send.reshape(-1), sums[n_bias:shared], sums[shared:]]))
    mod_got, rest = got[: mod_send.size].reshape(mod_send.shape), got[mod_send.size :]
    bias_sums = sums[:n_bias] + rest[2 * width :]
    out_sums = sums[n_bias:shared] + rest[: 2 * width]
    grad_mod = ordered(y_at, mod_keep[:, None], mod_got[:, None], 1).reshape(2 * dp_size, ada_cols)
    one_got = scatter_z(one_sends)
    owned_ada = lax.dot_general(
        silu_mine.astype(f32), after(grad_mod, one_sends), (((0,), (0,)), ((), ())), precision=highest
    )
    grad_ba = jnp.sum(grad_mod, axis=0)
    silu_part = lax.dot_general(
        after(grad_mod, one_sends), w_ada.astype(f32), (((1,), (1,)), ((), ())), precision=highest
    )
    silu_part = silu_part + swap_cores(silu_part)
    silu_part = silu_part + swap_y(silu_part)
    owned_one = add_all(one_keep, one_got)
    grad_silu = exchange_small(silu_part.reshape(dp_size, latents, ada_rows))
    cond_vals = condition.astype(f32)
    cond_sigmoid = jax.nn.sigmoid(cond_vals)
    grad_condition = grad_silu * cond_sigmoid * (1.0 + cond_vals * (1.0 - cond_sigmoid))
    return (
        result,
        grad_tokens,
        grad_condition,
        owned_ada,
        grad_ba,
        owned_one[:, :n_qkv],
        bias_sums[:n_bqv],
        owned_one[:, n_qkv:].T,
        out_sums[:width],
        add_all(fc1_keep, fc1_got),
        bias_sums[n_bqv:],
        add_all(fc2_keep, fc2_got).T,
        out_sums[width:],
    )


def solution(mesh):
    placed = (
        P(("dp", "tensor"), None),
        P("dp", None),
        P("dp", "tensor"),
        P("tensor"),
        P("dp", "tensor"),
        P("tensor"),
        P("tensor", "dp"),
        P(),
        P("dp", "tensor"),
        P("tensor"),
        P("tensor", "dp"),
        P(),
        P(("dp", "tensor"), None),
    )
    return jax.shard_map(
        shards,
        mesh=mesh,
        in_specs=placed,
        out_specs=(
            P(("dp", "tensor"), None),
            P(("dp", "tensor"), None),
            P("dp", None),
            P("dp", "tensor"),
            P("tensor"),
            P("dp", "tensor"),
            P("tensor"),
            P("tensor", "dp"),
            P(),
            P("dp", "tensor"),
            P("tensor"),
            P("tensor", "dp"),
            P(),
        ),
        check_vma=False,
    )
```
